256 devices in a mesh: src: 16 (over y, x_hi, core), tgt: 16 (over z, x_lo).
Axes of the slice: x: 4 (x_hi: 2, x_lo: 2; x = x_hi * 2 + x_lo), y: 4, z: 8, core: 2. Of those that a mesh axis runs over, the one named last changes fastest.
Arguments:
- edge_feat: bfloat16 [16, 16, 2048, 512], P('src', 'tgt'), may hold values from -6 to 6
- tile_counts: int32 [16, 16], P('src', 'tgt'), may hold values from 512 to 2048, as said below
- reverse_rows: int32 [16, 16, 2048], P('src', 'tgt'), may hold values from 0 to 2047, as said below
- incidence: int32 [16, 16, 2048], P('src', 'tgt'), may hold values from 0 to 4095
- owner_map: int32 [16, 16], P('tgt'), may hold values from 0 to 15, each once within a row
- w_pre: bfloat16 [3, 512, 512], replicated, may hold values from -0.25 to 0.25
- w_post: bfloat16 [3, 512, 512], replicated, may hold values from -0.25 to 0.25
- w_out: bfloat16 [512, 256], replicated, may hold values from -0.125 to 0.125
Outputs:
- atom_messages: bfloat16 [16, 4096, 256], P('tgt', 'src')
The draws below stay inside these ranges and needn't reach their ends.
Inputs may be any that keep to these rules, and one draw needn't show every extreme that they name: tile_counts[s, b] equals tile_counts[b, s]; some tile is full with 2048 live edges. For each tile (s, b), reverse_rows[s, b, :] is a permutation of the slots that maps live slots to live slots of tile (b, s). `owner_map`: each row is a permutation.
All inputs are finite; a program needn't handle non-finite values.
Results may differ from the reference program's by a relative error of at most 0.013.
Values may be sent and summed in bfloat16 or wider, within the bound.
A program may use at most 64 MiB of HBM per device.

```python
import math
import jax
import jax.numpy as jnp
import numpy as np
from jax import lax

W = 512
MESSAGE_WIDTH = 256
LAYERS = 3
ATOMS_BLK = 4096
ATOM_BLOCKS = 16
CAP = 2048
GROUP = 4096
SUBBLOCK_ATOMS = 256
N_TGT = 16


def shared_counts(key):
    folded = jax.random.fold_in(key, 7)
    first_key, second_key = jax.random.split(folded)
    raw_counts = jax.random.randint(first_key, (ATOM_BLOCKS, ATOM_BLOCKS), CAP // 4, CAP + 1)
    row_ids = lax.broadcasted_iota(jnp.int32, (ATOM_BLOCKS, ATOM_BLOCKS), 0)
    col_ids = lax.broadcasted_iota(jnp.int32, (ATOM_BLOCKS, ATOM_BLOCKS), 1)
    symmetric = jnp.where(row_ids <= col_ids, raw_counts, raw_counts.T)
    chosen = jax.random.randint(second_key, (), 0, ATOM_BLOCKS)
    return jnp.where((row_ids == chosen) & (col_ids == chosen), CAP, symmetric).astype(jnp.int32)


def draw_tile_counts(key, part):
    return shared_counts(key)


def draw_reverse_rows(key, part):
    counts = shared_counts(key)
    scores = jax.random.randint(jax.random.fold_in(key, 11), (ATOM_BLOCKS, ATOM_BLOCKS, CAP), 0, 4096)
    slot_ids = lax.broadcasted_iota(jnp.int32, (ATOM_BLOCKS, ATOM_BLOCKS, CAP), 2)
    mirror = counts.T[:, :, None]
    ordered_keys = scores * CAP + slot_ids + jnp.where(slot_ids >= mirror, 4096 * CAP, 0)
    return jnp.argsort(ordered_keys, axis=-1).astype(jnp.int32)


def with_ends(entries, key, low, largest):
    longest = entries.shape.index(max(entries.shape))
    spots = []
    for shift in (0, 1):
        where = [jax.random.randint(jax.random.fold_in(key, axis), (), 0, length) for axis, length in enumerate(entries.shape)]
        where[longest] = (where[longest] + shift) % entries.shape[longest]
        spots.append(tuple(where))
    return entries.at[spots[0]].set(low).at[spots[1]].set(largest)


def shard_levels(key, dims, cuts, least, top_value):
    def one(dim, parts):
        draws = jax.random.uniform(jax.random.fold_in(jax.random.fold_in(key, 6), dim), (parts,), jnp.float32, least / len(cuts), top_value / len(cuts))
        return jnp.repeat(jnp.exp(draws), dims[dim] // parts).reshape((-1,) + (1,) * (len(dims) - dim - 1))

    level = one(*cuts[0])
    for cut in cuts[1:]:
        level = level * one(*cut)
    return level


def rank_table(amount, skew):
    loads = [(1 << 20) // math.isqrt(grade ** skew) + 1 for grade in range(1, amount + 1)]
    scale = 1 + sum(loads) // (1 << 30)
    return np.cumsum(np.array([max(1, weight // scale) for weight in loads]))


def ranked_ids(stream_key, shape, number_of, lean):
    table = rank_table(number_of, lean)
    lot = jax.random.randint(jax.random.fold_in(stream_key, 1), shape, 0, int(table[number_of - 1]))
    grade = jnp.searchsorted(jnp.asarray(table, jnp.int32), lot, side="right")
    return jax.random.permutation(jax.random.fold_in(stream_key, 2), number_of)[grade].astype(jnp.int32)


def scatter_about(own_key, dims, spread, limit, pieces=(), kind=jnp.bfloat16):
    drawn = jax.random.normal(own_key, dims, jnp.float32) * spread
    if len(pieces) > 0:
        drawn = shard_levels(own_key, dims, pieces, -0.22, 0.18) * drawn
    return jnp.clip(drawn, min=-limit, max=limit).astype(kind)


def setup_inputs(seed: int = 0) -> dict:
    seeds = jax.random.split(jax.random.key(seed), 9)
    return {
        "edge_feat": scatter_about(seeds[0], (ATOM_BLOCKS, ATOM_BLOCKS, CAP, W), 1.0, 6.0, ((0, 16), (1, 16))),
        "tile_counts": draw_tile_counts(jax.random.fold_in(seeds[8], 71), 0),
        "reverse_rows": draw_reverse_rows(jax.random.fold_in(seeds[8], 71), 0),
        "incidence": with_ends(ranked_ids(seeds[3], (ATOM_BLOCKS, ATOM_BLOCKS, CAP), ATOMS_BLK, 1), jax.random.fold_in(seeds[3], 3), 0, ATOMS_BLK - 1).astype(jnp.int32),
        "owner_map": jax.vmap(lambda own: jax.random.permutation(own, ATOM_BLOCKS))(jax.random.split(seeds[4], N_TGT)).reshape((N_TGT, ATOM_BLOCKS)).astype(jnp.int32),
        "w_pre": scatter_about(seeds[5], (LAYERS, W, W), W ** -0.5, 0.25),
        "w_post": scatter_about(seeds[6], (LAYERS, W, W), W ** -0.5, 0.25),
        "w_out": scatter_about(seeds[7], (W, MESSAGE_WIDTH), (4 * W) ** -0.5, 0.125),
    }


HALF_ROOT = 0.7071067811865476


def residual_stack(hidden, weights):
    for layer_index in range(weights.shape[0]):
        projected_edges = jnp.dot(hidden, weights[layer_index], preferred_element_type=jnp.float32)
        hidden = ((hidden.astype(jnp.float32) + jax.nn.silu(projected_edges)) * HALF_ROOT).astype(jnp.bfloat16)
    return hidden


def reference(edge_feat, tile_counts, reverse_rows, incidence, owner_map, w_pre, w_post, w_out):
    first_pass = lax.map(lambda tile_group: residual_stack(tile_group.reshape(ATOM_BLOCKS * CAP, W), w_pre).reshape(ATOM_BLOCKS, CAP, W), edge_feat)
    slot_ids = lax.broadcasted_iota(jnp.int32, (ATOM_BLOCKS, CAP), 1)
    block_ids = lax.broadcasted_iota(jnp.int32, (ATOM_BLOCKS, CAP), 0)

    def accumulate(running, source_index):
        own_rows = first_pass[source_index]
        mirrored = first_pass[:, source_index]
        pulled = jax.vmap(lambda one_tile, ordering: one_tile[ordering])(mirrored, reverse_rows[source_index])
        joined = ((own_rows.astype(jnp.float32) + pulled.astype(jnp.float32)) * HALF_ROOT).astype(jnp.bfloat16)
        second_pass = residual_stack(joined.reshape(ATOM_BLOCKS * CAP, W), w_post)
        atom_message = jnp.dot(second_pass, w_out, preferred_element_type=jnp.float32).astype(jnp.bfloat16)
        live_rows = slot_ids < tile_counts[source_index][:, None]
        segment_ids = jnp.where(live_rows, block_ids * ATOMS_BLK + incidence[source_index], ATOM_BLOCKS * ATOMS_BLK).reshape(-1)
        added = jax.ops.segment_sum(atom_message.astype(jnp.float32), segment_ids, num_segments=ATOM_BLOCKS * ATOMS_BLK + 1)
        return running + added[:ATOM_BLOCKS * ATOMS_BLK], None

    block_summed, _ = lax.scan(accumulate, jnp.zeros((ATOM_BLOCKS * ATOMS_BLK, MESSAGE_WIDTH), jnp.float32), jnp.arange(ATOM_BLOCKS, dtype=jnp.int32))
    edge_groups = block_summed.reshape(N_TGT, ATOM_BLOCKS, SUBBLOCK_ATOMS, MESSAGE_WIDTH)
    inverse = jnp.argsort(owner_map, axis=1).astype(jnp.int32)
    ordered = jnp.take_along_axis(edge_groups, inverse[:, :, None, None], axis=1)
    return ordered.reshape(N_TGT, GROUP, MESSAGE_WIDTH).astype(jnp.bfloat16)
```

```python
import jax
import jax.numpy as jnp
from jax import lax
from jax.experimental import pallas as pl
from jax.experimental.pallas import tpu as pltpu
from jax.sharding import Mesh
from jax.sharding import PartitionSpec as P

SUB = 256
HALF_ROOT = 0.7071067811865476
MESH = pl.DeviceIdType.MESH
SRC = ("y", "xh", "c")
TGT = ("z", "xl")
CHUNKS = 8
LAG = 2
F32 = jnp.float32
BF16 = jnp.bfloat16


def layer(hidden, weight):
    half = jnp.dot(hidden, weight, preferred_element_type=F32) * 0.5
    silu = half + half * jnp.tanh(half)
    return ((hidden.astype(F32) + silu) * HALF_ROOT).astype(BF16)


def where_am_i():
    return tuple(lax.axis_index(name) for name in ("y", "xh", "c", "z", "xl"))


def mirror_kernel(
    edge_ref, w_ref, rev_ref, joined_ref,
    first, spread, moved, landed, total, rev_wide,
    send1, recv1, send2, recv2, send3, recv3,
):
    y, xh, c, z, xl = where_am_i()
    zy, z0 = z // 2, lax.rem(z, 2)
    alone = (xh == z0) & (xl == c)
    rows, width = edge_ref.shape
    chunk = rows // CHUNKS
    piece = chunk // 4

    def beside(step):
        return (lax.rem(y + step, 4), xh, c, z, xl)

    def across(step):
        return (y, z0, xl, 2 * lax.rem(zy + step, 4) + xh, c)

    barrier = pltpu.get_barrier_semaphore()
    for step in range(1, 4):
        pl.semaphore_signal(barrier, inc=1, device_id=beside(step), device_id_type=MESH)
        pl.semaphore_signal(barrier, inc=1, device_id=across(step), device_id_type=MESH)

    @pl.when(jnp.logical_not(alone))
    def _():
        pl.semaphore_signal(barrier, inc=1, device_id=across(0), device_id_type=MESH)

    def remote(src, dst, send, recv, device):
        return pltpu.make_async_remote_copy(
            src_ref=src, dst_ref=dst, send_sem=send, recv_sem=recv,
            device_id=device, device_id_type=MESH,
        )

    def copy1(g, step):
        start = pl.multiple_of(g * chunk + lax.rem(y + step, 4) * piece, piece)
        return remote(
            first.at[pl.ds(start, piece)], spread.at[g, step],
            send1.at[g, step], recv1.at[g, step], beside(step),
        )

    def copy2(g, step):
        held = lax.rem(y - zy - step + 8, 4)
        return remote(
            spread.at[g, held], moved.at[g, step],
            send2.at[g, step], recv2.at[g, step], across(step),
        )

    def stay2(g):
        held = lax.rem(y - zy + 8, 4)
        return pltpu.make_async_copy(spread.at[g, held], moved.at[g, 0], recv2.at[g, 0])

    def copy3(g, step):
        held = lax.rem(zy - y - step + 8, 4)
        return remote(
            moved.at[g, held], landed.at[g, step],
            send3.at[g, step], recv3.at[g, step], beside(step),
        )

    def embed(g):
        here = pl.ds(pl.multiple_of(g * chunk, chunk), chunk)
        hidden = edge_ref[here, :]
        for index in range(w_ref.shape[0]):
            hidden = layer(hidden, w_ref[index])
        first[here, :] = hidden

    def stage(i, carry):
        @pl.when(i < CHUNKS)
        def _():
            for step in range(1, 4):
                copy1(i, step).start()
            own = pl.ds(pl.multiple_of(i * chunk + y * piece, piece), piece)
            spread[i, 0] = first[own, :]

        @pl.when(i + 1 < CHUNKS)
        def _():
            embed(i + 1)

        @pl.when((i >= 1) & (i <= CHUNKS))
        def _():
            g = i - 1
            for step in range(1, 4):
                copy1(g, step).wait_recv()
            for step in range(1, 4):
                copy2(g, step).start()

            @pl.when(alone)
            def _():
                stay2(g).start()

            @pl.when(jnp.logical_not(alone))
            def _():
                copy2(g, 0).start()

        @pl.when((i >= 1 + LAG) & (i <= CHUNKS + LAG))
        def _():
            g = i - 1 - LAG
            for step in range(1, 4):
                copy2(g, step).wait_recv()

            @pl.when(alone)
            def _():
                stay2(g).wait()

            @pl.when(jnp.logical_not(alone))
            def _():
                copy2(g, 0).wait_recv()

            for step in range(1, 4):
                copy3(g, step).start()
            landed[g, 0] = moved[g, lax.rem(zy - y + 4, 4)]

        @pl.when(i == 1 + LAG)
        def _():
            total[...] = jnp.zeros_like(total)

        @pl.when(i >= 2 + LAG)
        def _():
            g = i - 2 - LAG
            for step in range(1, 4):
                copy3(g, step).wait_recv()
            block = landed[g].reshape(chunk, width)
            lane = lax.broadcasted_iota(jnp.int32, (1, chunk), 1)
            slot, offset = lane // piece, lane % piece
            origin = g * chunk + ((y + 4 - slot) % 4) * piece + offset

            def add(t, carry):
                some = pl.ds(pl.multiple_of(t * 256, 256), 256)
                picked = jnp.concatenate([rev_wide[some, :]] * (chunk // 128), axis=1)
                choose = jnp.where(picked == origin, 1.0, 0.0).astype(BF16)
                total[some, :] += jnp.dot(choose, block, preferred_element_type=F32)
                return carry

            lax.fori_loop(0, rows // 256, add, 0)

        return carry

    embed(0)

    def widen(t, carry):
        part = pl.ds(pl.multiple_of(t * 128, 128), 128)
        rev_wide[part, :] = jnp.broadcast_to(rev_ref[:, part], (128, 128)).T
        return carry

    lax.fori_loop(0, rows // 128, widen, 0)

    pl.semaphore_wait(barrier, jnp.where(alone, 6, 7))
    lax.fori_loop(0, CHUNKS + LAG + 2, stage, 0)

    def finish(g, carry):
        here = pl.ds(pl.multiple_of(g * chunk, chunk), chunk)
        both = first[here, :].astype(F32) + total[here, :]
        joined_ref[here, :] = (both * HALF_ROOT).astype(BF16)
        for step in range(1, 4):
            copy1(g, step).wait_send()
            copy2(g, step).wait_send()
            copy3(g, step).wait_send()

        @pl.when(jnp.logical_not(alone))
        def _():
            copy2(g, 0).wait_send()

        return carry

    lax.fori_loop(0, CHUNKS, finish, 0)


def mirror(edge, w_pre, rev):
    rows, width = edge.shape
    piece = rows // CHUNKS // 4
    pieces = pltpu.VMEM((CHUNKS, 4, piece, width), BF16)
    sems = pltpu.SemaphoreType.DMA((CHUNKS, 4))
    vmem = pl.BlockSpec(memory_space=pltpu.VMEM)
    return pl.pallas_call(
        mirror_kernel,
        name="mirror",
        out_shape=jax.ShapeDtypeStruct((rows, width), BF16),
        in_specs=[vmem] * 3,
        out_specs=vmem,
        scratch_shapes=[
            pltpu.VMEM((rows, width), BF16),
            pieces, pieces, pieces,
            pltpu.VMEM((rows, width), F32),
            pltpu.VMEM((rows, 128), jnp.int32),
            sems, sems, sems, sems, sems, sems,
        ],
        compiler_params=pltpu.CompilerParams(
            collective_id=0, has_side_effects=True, vmem_limit_bytes=40 << 20
        ),
    )(edge, w_pre, rev)


def message_kernel(joined_ref, w_ref, w_out_ref, message_ref):
    hidden = joined_ref[...]
    for index in range(w_ref.shape[0]):
        hidden = layer(hidden, w_ref[index])
    message_ref[...] = jnp.dot(hidden, w_out_ref[...], preferred_element_type=F32).astype(BF16)


def messages(joined, w_post, w_out):
    rows, width = joined.shape
    tile = 512
    return pl.pallas_call(
        message_kernel,
        name="messages",
        grid=(rows // tile,),
        out_shape=jax.ShapeDtypeStruct((rows, w_out.shape[1]), BF16),
        in_specs=[
            pl.BlockSpec((tile, width), lambda i: (i, 0)),
            pl.BlockSpec(w_post.shape, lambda i: (0, 0, 0)),
            pl.BlockSpec(w_out.shape, lambda i: (0, 0)),
        ],
        out_specs=pl.BlockSpec((tile, w_out.shape[1]), lambda i: (i, 0)),
        compiler_params=pltpu.CompilerParams(vmem_limit_bytes=24 << 20),
    )(joined, w_post, w_out)


HOPS = ((2, 1), (1, 1), (3, 1), (2, 0), (0, 1), (1, 0), (3, 0), (0, 0))


def reduce_kernel(
    message_ref, atom_ref, count_ref, owner_ref, out_ref,
    target, mine, pair_out, pair_in, far_out, far_in,
    pair_send, pair_recv, far_send, far_recv,
):
    y, xh, c, z, xl = where_am_i()
    edges, width = message_ref.shape
    other = (y, xh, 1 - c, z, xl)

    def owner_of(hop):
        return lax.rem(y + HOPS[hop][0], 4), lax.rem(xh + HOPS[hop][1], 2)

    def far_device(hop):
        return (*owner_of(hop), c, z, xl)

    barrier = pltpu.get_barrier_semaphore()
    pl.semaphore_signal(barrier, inc=1, device_id=other, device_id_type=MESH)
    for hop in range(7):
        pl.semaphore_signal(barrier, inc=1, device_id=far_device(hop), device_id_type=MESH)

    atoms = atom_ref[...]
    block = atoms // SUB
    place = jnp.zeros_like(atoms)
    for k in range(owner_ref.shape[1]):
        place = jnp.where(block == k, owner_ref[0, k], place)
    slot = lax.broadcasted_iota(jnp.int32, atoms.shape, 1)
    target[...] = jnp.where(slot < count_ref[0, 0], place * SUB + atoms % SUB, -1)
    pl.semaphore_wait(barrier, 8)

    row = lax.broadcasted_iota(jnp.int32, (SUB, edges), 0)

    def part(position):
        select = jnp.where(row == target[...] - position * SUB, 1.0, 0.0).astype(BF16)
        return jnp.dot(select, message_ref[...], preferred_element_type=F32)

    def pair_copy(hop):
        return pltpu.make_async_remote_copy(
            src_ref=pair_out.at[hop], dst_ref=pair_in.at[hop],
            send_sem=pair_send.at[hop], recv_sem=pair_recv.at[hop],
            device_id=other, device_id_type=MESH,
        )

    def far_copy(hop):
        return pltpu.make_async_remote_copy(
            src_ref=far_out.at[hop], dst_ref=far_in.at[hop],
            send_sem=far_send.at[hop], recv_sem=far_recv.at[hop],
            device_id=far_device(hop), device_id_type=MESH,
        )

    def send_on(hop):
        pair_copy(hop).wait_recv()
        chip_sum = mine[hop % 2] + pair_in[hop].astype(F32)
        if hop < 7:
            far_out[hop] = chip_sum.astype(BF16)
            far_copy(hop).start()
            return None
        return chip_sum

    for hop in range(8):
        to_y, to_xh = owner_of(hop)
        position = 4 * to_y + 2 * to_xh
        pair_out[hop] = part(position + 1 - c).astype(BF16)
        pair_copy(hop).start()
        mine[hop % 2] = part(position + c)
        if hop > 0:
            send_on(hop - 1)
    result = send_on(7)
    for hop in range(7):
        far_copy(hop).wait_recv()
        result = result + far_in[hop].astype(F32)
    out_ref[...] = result.astype(BF16)
    for hop in range(8):
        pair_copy(hop).wait_send()
    for hop in range(7):
        far_copy(hop).wait_send()


def reduce_to_owner(message, atoms, count, owners):
    width = message.shape[1]
    blocks = lambda n: pltpu.VMEM((n, SUB, width), BF16)
    sems = pltpu.SemaphoreType.DMA((8,))
    vmem = pl.BlockSpec(memory_space=pltpu.VMEM)
    smem = pl.BlockSpec(memory_space=pltpu.SMEM)
    return pl.pallas_call(
        reduce_kernel,
        name="reduce_to_owner",
        out_shape=jax.ShapeDtypeStruct((SUB, width), BF16),
        in_specs=[vmem, vmem, smem, smem],
        out_specs=vmem,
        scratch_shapes=[
            pltpu.VMEM(atoms.shape, jnp.int32),
            pltpu.VMEM((2, SUB, width), F32),
            blocks(8), blocks(8), blocks(7), blocks(7),
            sems, sems, sems, sems,
        ],
        compiler_params=pltpu.CompilerParams(
            collective_id=1, has_side_effects=True, vmem_limit_bytes=24 << 20
        ),
    )(message, atoms, count, owners)


def shards(edge_feat, tile_counts, reverse_rows, incidence, owner_map, w_pre, w_post, w_out):
    joined = mirror(edge_feat[0, 0], w_pre, reverse_rows[0])
    message = messages(joined, w_post, w_out)
    return reduce_to_owner(message, incidence[0], tile_counts, owner_map)[None]


def solution(mesh):
    finer = Mesh(mesh.devices.reshape(4, 2, 2, 8, 2), ("y", "xh", "c", "z", "xl"))
    return jax.shard_map(
        shards,
        mesh=finer,
        in_specs=(
            P(SRC, TGT, None, None),
            P(SRC, TGT),
            P(SRC, TGT, None),
            P(SRC, TGT, None),
            P(TGT, None),
            P(),
            P(),
            P(),
        ),
        out_specs=P(TGT, SRC, None),
        check_vma=False,
    )
```

```python
import jax
import jax.numpy as jnp
from jax import lax
from jax.experimental import pallas as pl
from jax.experimental.pallas import tpu as pltpu
from jax.sharding import Mesh
from jax.sharding import PartitionSpec as P

SUB = 256
HALF_ROOT = 0.7071067811865476
MESH = pl.DeviceIdType.MESH
SRC = ("y", "xh", "c")
TGT = ("z", "xl")
CHUNKS = 8
LAG = 2
F32 = jnp.float32
BF16 = jnp.bfloat16


def layer(hidden, weight):
    half = jnp.dot(hidden, weight, preferred_element_type=F32) * 0.5
    silu = half + half * jnp.tanh(half)
    return ((hidden.astype(F32) + silu) * HALF_ROOT).astype(BF16)


def where_am_i():
    return tuple(lax.axis_index(name) for name in ("y", "xh", "c", "z", "xl"))


def mirror_kernel(
    edge_ref, w_ref, rev_ref, joined_ref,
    first, spread, midway, moved, landed, total, rev_wide,
    send1, recv1, send2, recv2, send3, recv3, send4, recv4,
):
    y, xh, c, z, xl = where_am_i()
    zy, z0 = z // 2, lax.rem(z, 2)
    odd = lax.rem(xh + z0, 2)
    relay = odd == 0
    settled = c == xl
    alone = relay & settled
    far = jnp.logical_not(alone)
    leaf = jnp.logical_not(relay)
    rows, width = edge_ref.shape
    chunk = rows // CHUNKS
    piece = chunk // 4

    def along_y(step):
        return (lax.rem(y + step, 4), xh, c, z, xl)

    def along_z(step):
        return (y, xh, c, lax.rem(z + step, 8), xl)

    def along_x(flip):
        return (y, lax.rem(xh + flip, 2), xl, z, c)

    def greet(device):
        pl.semaphore_signal(barrier, inc=1, device_id=device, device_id_type=MESH)

    barrier = pltpu.get_barrier_semaphore()
    for step in range(1, 4):
        greet(along_y(step))
    for step in range(1, 8):
        greet(along_z(step))
    greet(along_x(1))

    @pl.when(jnp.logical_not(settled))
    def _():
        greet(along_x(0))

    def remote(src, dst, send, recv, device):
        return pltpu.make_async_remote_copy(
            src_ref=src, dst_ref=dst, send_sem=send, recv_sem=recv,
            device_id=device, device_id_type=MESH,
        )

    def when(condition, work):
        if condition is True:
            work()
        else:
            pl.when(condition)(work)

    def copy1(g, step):
        start = pl.multiple_of(g * chunk + lax.rem(y + step, 4) * piece, piece)
        return remote(
            first.at[pl.ds(start, piece)], spread.at[g, step],
            send1.at[g, step], recv1.at[g, step], along_y(step),
        )

    def hop2(m):
        return 2 * m + odd

    def held2(m):
        return lax.rem(y + 8 - lax.rem(z + hop2(m), 8) // 2, 4)

    def copy2(x_first, g, m):
        return remote(
            spread.at[g, held2(m)], midway.at[g, hop2(m)],
            send2.at[g, m], recv2.at[g, hop2(m)],
            along_x(odd) if x_first else along_z(hop2(m)),
        )

    def far2(x_first, m):
        return far if x_first else (leaf if m == 0 else True)

    def near2(x_first, m):
        return alone if x_first else (relay if m == 0 else False)

    def slot3(x_first, hop):
        turn = z0 if x_first else 1 - z0
        return lax.rem((hop + (hop % 2) * turn) // 2, 4)

    def copy3(x_first, g, hop):
        return remote(
            midway.at[g, hop], moved.at[g, slot3(x_first, hop)],
            send3.at[g, hop], recv3.at[g, slot3(x_first, hop)],
            along_z(hop) if x_first else along_x(hop % 2),
        )

    def far3(x_first, hop):
        if x_first:
            return relay if hop else False
        return relay if hop % 2 else relay & far

    def near3(x_first, hop):
        if x_first:
            return False if hop else relay
        return False if hop % 2 else alone

    def got2(g, hop):
        return remote(
            spread.at[g, 0], midway.at[g, hop], send2.at[g, 0], recv2.at[g, hop], along_y(1)
        )

    def got3(g, slot):
        return remote(
            midway.at[g, 0], moved.at[g, slot], send3.at[g, 0], recv3.at[g, slot], along_y(1)
        )

    def copy4(g, step):
        held = lax.rem(zy - y - step + 8, 4)
        return remote(
            moved.at[g, held], landed.at[g, step],
            send4.at[g, step], recv4.at[g, step], along_y(step),
        )

    def embed(g):
        here = pl.ds(pl.multiple_of(g * chunk, chunk), chunk)
        hidden = edge_ref[here, :]
        for index in range(w_ref.shape[0]):
            hidden = layer(hidden, w_ref[index])
        first[here, :] = hidden

    def second_leg(x_first, g):
        for step in range(1, 4):
            copy1(g, step).wait_recv()
        for m in range(4):
            if far2(x_first, m) is not False:
                when(far2(x_first, m), lambda: copy2(x_first, g, m).start())
            if near2(x_first, m) is not False:

                def keep():
                    midway[g, hop2(m)] = spread[g, held2(m)]

                when(near2(x_first, m), keep)

    def third_leg(x_first, g):
        def arrive():
            for hop in range(8):
                if x_first:
                    when(True if hop % 2 else far, lambda: got2(g, hop).wait_recv())
                elif hop:
                    got2(g, hop).wait_recv()

        when(relay, arrive)
        for hop in (4, 3, 5, 2, 6, 1, 7, 0):
            if far3(x_first, hop) is not False:
                when(far3(x_first, hop), lambda: copy3(x_first, g, hop).start())
            if near3(x_first, hop) is not False:

                def keep():
                    moved[g, slot3(x_first, hop)] = midway[g, hop]

                when(near3(x_first, hop), keep)

    def fourth_leg(x_first, g):
        for slot in range(4):
            if x_first:
                when(True if slot else leaf, lambda: got3(g, slot).wait_recv())
            else:
                when(far, lambda: got3(g, slot).wait_recv())

    def by_kind(work, g):
        @pl.when(lax.rem(g, 2) == 0)
        def _():
            work(False, g)

        @pl.when(lax.rem(g, 2) == 1)
        def _():
            work(True, g)

    def stage(i, carry):
        @pl.when(i < CHUNKS)
        def _():
            for step in range(1, 4):
                copy1(i, step).start()
            own = pl.ds(pl.multiple_of(i * chunk + y * piece, piece), piece)
            spread[i, 0] = first[own, :]

        @pl.when(i + 1 < CHUNKS)
        def _():
            embed(i + 1)

        @pl.when((i >= 1) & (i <= CHUNKS))
        def _():
            by_kind(second_leg, i - 1)

        @pl.when((i >= 1 + LAG) & (i <= CHUNKS + LAG))
        def _():
            by_kind(third_leg, i - 1 - LAG)

        @pl.when(i == 1 + LAG)
        def _():
            total[...] = jnp.zeros_like(total)

        @pl.when((i >= 1 + 2 * LAG) & (i <= CHUNKS + 2 * LAG))
        def _():
            g = i - 1 - 2 * LAG
            by_kind(fourth_leg, g)
            for step in range(1, 4):
                copy4(g, step).start()
            landed[g, 0] = moved[g, lax.rem(zy - y + 4, 4)]

        @pl.when(i >= 2 + 2 * LAG)
        def _():
            g = i - 2 - 2 * LAG
            for step in range(1, 4):
                copy4(g, step).wait_recv()
            block = landed[g].reshape(chunk, width)
            lane = lax.broadcasted_iota(jnp.int32, (1, chunk), 1)
            slot, offset = lane // piece, lane % piece
            origin = g * chunk + ((y + 4 - slot) % 4) * piece + offset

            def add(t, carry):
                some = pl.ds(pl.multiple_of(t * 256, 256), 256)
                picked = jnp.concatenate([rev_wide[some, :]] * (chunk // 128), axis=1)
                choose = jnp.where(picked == origin, 1.0, 0.0).astype(BF16)
                total[some, :] += jnp.dot(choose, block, preferred_element_type=F32)
                return carry

            lax.fori_loop(0, rows // 256, add, 0)

        return carry

    embed(0)

    def widen(t, carry):
        part = pl.ds(pl.multiple_of(t * 128, 128), 128)
        rev_wide[part, :] = jnp.broadcast_to(rev_ref[:, part], (128, 128)).T
        return carry

    lax.fori_loop(0, rows // 128, widen, 0)
    pl.semaphore_wait(barrier, jnp.where(settled, 11, 12))
    lax.fori_loop(0, CHUNKS + 2 * LAG + 2, stage, 0)

    def sent(x_first, g):
        for m in range(4):
            when(far2(x_first, m), lambda: copy2(x_first, g, m).wait_send())
        for hop in range(8):
            if far3(x_first, hop) is not False:
                when(far3(x_first, hop), lambda: copy3(x_first, g, hop).wait_send())

    def finish(g, carry):
        here = pl.ds(pl.multiple_of(g * chunk, chunk), chunk)
        both = first[here, :].astype(F32) + total[here, :]
        joined_ref[here, :] = (both * HALF_ROOT).astype(BF16)
        for step in range(1, 4):
            copy1(g, step).wait_send()
            copy4(g, step).wait_send()
        by_kind(sent, g)
        return carry

    lax.fori_loop(0, CHUNKS, finish, 0)


def mirror(edge, w_pre, rev):
    rows, width = edge.shape
    piece = rows // CHUNKS // 4
    pieces = lambda n: pltpu.VMEM((CHUNKS, n, piece, width), BF16)
    sems = lambda n: pltpu.SemaphoreType.DMA((CHUNKS, n))
    vmem = pl.BlockSpec(memory_space=pltpu.VMEM)
    return pl.pallas_call(
        mirror_kernel,
        name="mirror",
        out_shape=jax.ShapeDtypeStruct((rows, width), BF16),
        in_specs=[vmem] * 3,
        out_specs=vmem,
        scratch_shapes=[
            pltpu.VMEM((rows, width), BF16),
            pieces(4), pieces(8), pieces(4), pieces(4),
            pltpu.VMEM((rows, width), F32),
            pltpu.VMEM((rows, 128), jnp.int32),
            sems(4), sems(4), sems(4), sems(8), sems(8), sems(4), sems(4), sems(4),
        ],
        compiler_params=pltpu.CompilerParams(
            collective_id=0, has_side_effects=True, vmem_limit_bytes=40 << 20
        ),
    )(edge, w_pre, rev)


def message_kernel(joined_ref, w_ref, w_out_ref, message_ref):
    hidden = joined_ref[...]
    for index in range(w_ref.shape[0]):
        hidden = layer(hidden, w_ref[index])
    message_ref[...] = jnp.dot(hidden, w_out_ref[...], preferred_element_type=F32).astype(BF16)


def messages(joined, w_post, w_out):
    rows, width = joined.shape
    tile = 512
    return pl.pallas_call(
        message_kernel,
        name="messages",
        grid=(rows // tile,),
        out_shape=jax.ShapeDtypeStruct((rows, w_out.shape[1]), BF16),
        in_specs=[
            pl.BlockSpec((tile, width), lambda i: (i, 0)),
            pl.BlockSpec(w_post.shape, lambda i: (0, 0, 0)),
            pl.BlockSpec(w_out.shape, lambda i: (0, 0)),
        ],
        out_specs=pl.BlockSpec((tile, w_out.shape[1]), lambda i: (i, 0)),
        compiler_params=pltpu.CompilerParams(vmem_limit_bytes=24 << 20),
    )(joined, w_post, w_out)


HOPS = ((2, 1), (1, 1), (3, 1), (2, 0), (0, 1), (1, 0), (3, 0), (0, 0))


def reduce_kernel(
    message_ref, atom_ref, count_ref, owner_ref, out_ref,
    target, mine, pair_out, pair_in, far_out, far_in,
    pair_send, pair_recv, far_send, far_recv,
):
    y, xh, c, z, xl = where_am_i()
    edges, width = message_ref.shape
    other = (y, xh, 1 - c, z, xl)

    def owner_of(hop):
        return lax.rem(y + HOPS[hop][0], 4), lax.rem(xh + HOPS[hop][1], 2)

    def far_device(hop):
        return (*owner_of(hop), c, z, xl)

    barrier = pltpu.get_barrier_semaphore()
    pl.semaphore_signal(barrier, inc=1, device_id=other, device_id_type=MESH)
    for hop in range(7):
        pl.semaphore_signal(barrier, inc=1, device_id=far_device(hop), device_id_type=MESH)

    atoms = atom_ref[...]
    block = atoms // SUB
    place = jnp.zeros_like(atoms)
    for k in range(owner_ref.shape[1]):
        place = jnp.where(block == k, owner_ref[0, k], place)
    slot = lax.broadcasted_iota(jnp.int32, atoms.shape, 1)
    target[...] = jnp.where(slot < count_ref[0, 0], place * SUB + atoms % SUB, -1)
    pl.semaphore_wait(barrier, 8)

    row = lax.broadcasted_iota(jnp.int32, (SUB, edges), 0)

    def part(position):
        select = jnp.where(row == target[...] - position * SUB, 1.0, 0.0).astype(BF16)
        return jnp.dot(select, message_ref[...], preferred_element_type=F32)

    def pair_copy(hop):
        return pltpu.make_async_remote_copy(
            src_ref=pair_out.at[hop], dst_ref=pair_in.at[hop],
            send_sem=pair_send.at[hop], recv_sem=pair_recv.at[hop],
            device_id=other, device_id_type=MESH,
        )

    def far_copy(hop):
        return pltpu.make_async_remote_copy(
            src_ref=far_out.at[hop], dst_ref=far_in.at[hop],
            send_sem=far_send.at[hop], recv_sem=far_recv.at[hop],
            device_id=far_device(hop), device_id_type=MESH,
        )

    def send_on(hop):
        pair_copy(hop).wait_recv()
        chip_sum = mine[hop % 2] + pair_in[hop].astype(F32)
        if hop < 7:
            far_out[hop] = chip_sum.astype(BF16)
            far_copy(hop).start()
            return None
        return chip_sum

    for hop in range(8):
        to_y, to_xh = owner_of(hop)
        position = 4 * to_y + 2 * to_xh
        pair_out[hop] = part(position + 1 - c).astype(BF16)
        pair_copy(hop).start()
        mine[hop % 2] = part(position + c)
        if hop > 0:
            send_on(hop - 1)
    result = send_on(7)
    for hop in range(7):
        far_copy(hop).wait_recv()
        result = result + far_in[hop].astype(F32)
    out_ref[...] = result.astype(BF16)
    for hop in range(8):
        pair_copy(hop).wait_send()
    for hop in range(7):
        far_copy(hop).wait_send()


def reduce_to_owner(message, atoms, count, owners):
    width = message.shape[1]
    blocks = lambda n: pltpu.VMEM((n, SUB, width), BF16)
    sems = pltpu.SemaphoreType.DMA((8,))
    vmem = pl.BlockSpec(memory_space=pltpu.VMEM)
    smem = pl.BlockSpec(memory_space=pltpu.SMEM)
    return pl.pallas_call(
        reduce_kernel,
        name="reduce_to_owner",
        out_shape=jax.ShapeDtypeStruct((SUB, width), BF16),
        in_specs=[vmem, vmem, smem, smem],
        out_specs=vmem,
        scratch_shapes=[
            pltpu.VMEM(atoms.shape, jnp.int32),
            pltpu.VMEM((2, SUB, width), F32),
            blocks(8), blocks(8), blocks(7), blocks(7),
            sems, sems, sems, sems,
        ],
        compiler_params=pltpu.CompilerParams(
            collective_id=1, has_side_effects=True, vmem_limit_bytes=24 << 20
        ),
    )(message, atoms, count, owners)


def shards(edge_feat, tile_counts, reverse_rows, incidence, owner_map, w_pre, w_post, w_out):
    joined = mirror(edge_feat[0, 0], w_pre, reverse_rows[0])
    message = messages(joined, w_post, w_out)
    return reduce_to_owner(message, incidence[0], tile_counts, owner_map)[None]


def solution(mesh):
    finer = Mesh(mesh.devices.reshape(4, 2, 2, 8, 2), ("y", "xh", "c", "z", "xl"))
    return jax.shard_map(
        shards,
        mesh=finer,
        in_specs=(
            P(SRC, TGT, None, None),
            P(SRC, TGT),
            P(SRC, TGT, None),
            P(SRC, TGT, None),
            P(TGT, None),
            P(),
            P(),
            P(),
        ),
        out_specs=P(TGT, SRC, None),
        check_vma=False,
    )
```

```python
import jax
import jax.numpy as jnp
from jax import lax
from jax.experimental import pallas as pl
from jax.experimental.pallas import tpu as pltpu
from jax.sharding import Mesh
from jax.sharding import PartitionSpec as P

SUB = 256
HALF_ROOT = 0.7071067811865476
MESH = pl.DeviceIdType.MESH
SRC = ("y", "xh", "c")
TGT = ("z", "xl")
CHUNKS = 8
LAGS = (2, 2, 2, 2)
F32 = jnp.float32
BF16 = jnp.bfloat16


def layer(hidden, weight):
    half = jnp.dot(hidden, weight, preferred_element_type=F32) * 0.5
    silu = half + half * jnp.tanh(half)
    return ((hidden.astype(F32) + silu) * HALF_ROOT).astype(BF16)


def where_am_i():
    return tuple(lax.axis_index(name) for name in ("y", "xh", "c", "z", "xl"))


def mirror_kernel(
    edge_ref, w_ref, rev_ref, joined_ref,
    first, spread, midway, moved, landed, total, rev_wide,
    send1, recv1, send2, recv2, send3, recv3, send4, recv4,
):
    y, xh, c, z, xl = where_am_i()
    zy, z0 = z // 2, lax.rem(z, 2)
    odd = lax.rem(xh + z0, 2)
    relay = odd == 0
    settled = c == xl
    alone = relay & settled
    far = jnp.logical_not(alone)
    leaf = jnp.logical_not(relay)
    rows, width = edge_ref.shape
    chunk = rows // CHUNKS
    piece = chunk // 4

    def along_y(step):
        return (lax.rem(y + step, 4), xh, c, z, xl)

    def along_z(step):
        return (y, xh, c, lax.rem(z + step, 8), xl)

    def along_x(flip):
        return (y, lax.rem(xh + flip, 2), xl, z, c)

    def greet(device):
        pl.semaphore_signal(barrier, inc=1, device_id=device, device_id_type=MESH)

    barrier = pltpu.get_barrier_semaphore()
    for step in range(1, 4):
        greet(along_y(step))
    for step in range(1, 8):
        greet(along_z(step))
    greet(along_x(1))

    @pl.when(jnp.logical_not(settled))
    def _():
        greet(along_x(0))

    def remote(src, dst, send, recv, device):
        return pltpu.make_async_remote_copy(
            src_ref=src, dst_ref=dst, send_sem=send, recv_sem=recv,
            device_id=device, device_id_type=MESH,
        )

    def when(condition, work):
        if condition is True:
            work()
        else:
            pl.when(condition)(work)

    def copy1(g, step):
        start = pl.multiple_of(g * chunk + lax.rem(y + step, 4) * piece, piece)
        return remote(
            first.at[pl.ds(start, piece)], spread.at[g, step],
            send1.at[g, step], recv1.at[g, step], along_y(step),
        )

    def hop2(m):
        return 2 * m + odd

    def held2(m):
        return lax.rem(y + 8 - lax.rem(z + hop2(m), 8) // 2, 4)

    def copy2(x_first, g, m):
        return remote(
            spread.at[g, held2(m)], midway.at[g, hop2(m)],
            send2.at[g, m], recv2.at[g, hop2(m)],
            along_x(odd) if x_first else along_z(hop2(m)),
        )

    def far2(x_first, m):
        return far if x_first else (leaf if m == 0 else True)

    def near2(x_first, m):
        return alone if x_first else (relay if m == 0 else False)

    def slot3(x_first, hop):
        turn = z0 if x_first else 1 - z0
        return lax.rem((hop + (hop % 2) * turn) // 2, 4)

    def copy3(x_first, g, hop):
        return remote(
            midway.at[g, hop], moved.at[g, slot3(x_first, hop)],
            send3.at[g, hop], recv3.at[g, slot3(x_first, hop)],
            along_z(hop) if x_first else along_x(hop % 2),
        )

    def far3(x_first, hop):
        if x_first:
            return relay if hop else False
        return relay if hop % 2 else relay & far

    def near3(x_first, hop):
        if x_first:
            return False if hop else relay
        return False if hop % 2 else alone

    def got2(g, hop):
        return remote(
            spread.at[g, 0], midway.at[g, hop], send2.at[g, 0], recv2.at[g, hop], along_y(1)
        )

    def got3(g, slot):
        return remote(
            midway.at[g, 0], moved.at[g, slot], send3.at[g, 0], recv3.at[g, slot], along_y(1)
        )

    def copy4(g, step):
        held = lax.rem(zy - y - step + 8, 4)
        return remote(
            moved.at[g, held], landed.at[g, step],
            send4.at[g, step], recv4.at[g, step], along_y(step),
        )

    def embed(g):
        here = pl.ds(pl.multiple_of(g * chunk, chunk), chunk)
        hidden = edge_ref[here, :]
        for index in range(w_ref.shape[0]):
            hidden = layer(hidden, w_ref[index])
        first[here, :] = hidden

    def second_leg(x_first, g):
        for step in range(1, 4):
            copy1(g, step).wait_recv()
        for m in range(4):
            if far2(x_first, m) is not False:
                when(far2(x_first, m), lambda: copy2(x_first, g, m).start())
            if near2(x_first, m) is not False:

                def keep():
                    midway[g, hop2(m)] = spread[g, held2(m)]

                when(near2(x_first, m), keep)

    def third_leg(x_first, g):
        def arrive():
            for hop in range(8):
                if x_first:
                    when(True if hop % 2 else far, lambda: got2(g, hop).wait_recv())
                elif hop:
                    got2(g, hop).wait_recv()

        when(relay, arrive)
        for hop in (4, 3, 5, 2, 6, 1, 7, 0):
            if far3(x_first, hop) is not False:
                when(far3(x_first, hop), lambda: copy3(x_first, g, hop).start())
            if near3(x_first, hop) is not False:

                def keep():
                    moved[g, slot3(x_first, hop)] = midway[g, hop]

                when(near3(x_first, hop), keep)

    def fourth_leg(x_first, g):
        for slot in range(4):
            if x_first:
                when(True if slot else leaf, lambda: got3(g, slot).wait_recv())
            else:
                when(far, lambda: got3(g, slot).wait_recv())

    def by_kind(work, g):
        @pl.when(lax.rem(g, 2) == 0)
        def _():
            work(False, g)

        @pl.when(lax.rem(g, 2) == 1)
        def _():
            work(True, g)

    def stage(i, carry):
        @pl.when(i < CHUNKS)
        def _():
            for step in range(1, 4):
                copy1(i, step).start()
            own = pl.ds(pl.multiple_of(i * chunk + y * piece, piece), piece)
            spread[i, 0] = first[own, :]

        @pl.when(i + 1 < CHUNKS)
        def _():
            embed(i + 1)

        for g, leg in ((i - LAGS[0], second_leg), (i - sum(LAGS[:2]), third_leg)):

            @pl.when((g >= 0) & (g < CHUNKS))
            def _():
                by_kind(leg, g)

        @pl.when(i == 2)
        def _():
            total[...] = jnp.zeros_like(total)

        g = i - sum(LAGS[:3])

        @pl.when((g >= 0) & (g < CHUNKS))
        def _():
            by_kind(fourth_leg, g)
            for step in range(1, 4):
                copy4(g, step).start()
            landed[g, 0] = moved[g, lax.rem(zy - y + 4, 4)]

        @pl.when(i >= sum(LAGS))
        def _():
            g = i - sum(LAGS)
            for step in range(1, 4):
                copy4(g, step).wait_recv()
            block = landed[g].reshape(chunk, width)
            lane = lax.broadcasted_iota(jnp.int32, (1, chunk), 1)
            slot, offset = lane // piece, lane % piece
            origin = g * chunk + ((y + 4 - slot) % 4) * piece + offset

            def add(t, carry):
                some = pl.ds(pl.multiple_of(t * 256, 256), 256)
                picked = jnp.concatenate([rev_wide[some, :]] * (chunk // 128), axis=1)
                choose = jnp.where(picked == origin, 1.0, 0.0).astype(BF16)
                total[some, :] += jnp.dot(choose, block, preferred_element_type=F32)
                return carry

            lax.fori_loop(0, rows // 256, add, 0)

        return carry

    embed(0)

    def widen(t, carry):
        part = pl.ds(pl.multiple_of(t * 128, 128), 128)
        rev_wide[part, :] = jnp.broadcast_to(rev_ref[:, part], (128, 128)).T
        return carry

    lax.fori_loop(0, rows // 128, widen, 0)
    pl.semaphore_wait(barrier, jnp.where(settled, 11, 12))
    lax.fori_loop(0, CHUNKS + sum(LAGS), stage, 0)

    def sent(x_first, g):
        for m in range(4):
            when(far2(x_first, m), lambda: copy2(x_first, g, m).wait_send())
        for hop in range(8):
            if far3(x_first, hop) is not False:
                when(far3(x_first, hop), lambda: copy3(x_first, g, hop).wait_send())

    def finish(g, carry):
        here = pl.ds(pl.multiple_of(g * chunk, chunk), chunk)
        both = first[here, :].astype(F32) + total[here, :]
        joined_ref[here, :] = (both * HALF_ROOT).astype(BF16)
        for step in range(1, 4):
            copy1(g, step).wait_send()
            copy4(g, step).wait_send()
        by_kind(sent, g)
        return carry

    lax.fori_loop(0, CHUNKS, finish, 0)


def mirror(edge, w_pre, rev):
    rows, width = edge.shape
    piece = rows // CHUNKS // 4
    pieces = lambda n: pltpu.VMEM((CHUNKS, n, piece, width), BF16)
    sems = lambda n: pltpu.SemaphoreType.DMA((CHUNKS, n))
    vmem = pl.BlockSpec(memory_space=pltpu.VMEM)
    return pl.pallas_call(
        mirror_kernel,
        name="mirror",
        out_shape=jax.ShapeDtypeStruct((rows, width), BF16),
        in_specs=[vmem] * 3,
        out_specs=vmem,
        scratch_shapes=[
            pltpu.VMEM((rows, width), BF16),
            pieces(4), pieces(8), pieces(4), pieces(4),
            pltpu.VMEM((rows, width), F32),
            pltpu.VMEM((rows, 128), jnp.int32),
            sems(4), sems(4), sems(4), sems(8), sems(8), sems(4), sems(4), sems(4),
        ],
        compiler_params=pltpu.CompilerParams(
            collective_id=0, has_side_effects=True, vmem_limit_bytes=40 << 20
        ),
    )(edge, w_pre, rev)


HOPS = ((2, 1), (1, 1), (3, 1), (0, 1), (2, 0), (1, 0), (3, 0), (0, 0))


def owner_kernel(
    joined_ref, w_ref, w_out_ref, atom_ref, count_ref, owner_ref, out_ref,
    message, match, place, pair_out, pair_in, mine,
    left_y_out, left_y_in, left_x_out, left_x_in, left_keep,
    right_x_out, right_x_in, right_y_out, right_y_in, right_keep,
    pair_send, pair_recv, left_y_send, left_y_recv, left_x_send, left_x_recv,
    right_x_send, right_x_recv, right_y_send, right_y_recv,
):
    y, xh, c, z, xl = where_am_i()
    edges, width = message.shape
    half = width // 2
    other = (y, xh, 1 - c, z, xl)
    across = (y, 1 - xh, c, z, xl)

    def along_y(step):
        return (lax.rem(y + step, 4), xh, c, z, xl)

    barrier = pltpu.get_barrier_semaphore()
    for device in (other, across, along_y(1), along_y(2), along_y(3)):
        pl.semaphore_signal(barrier, inc=1, device_id=device, device_id_type=MESH)

    atoms = atom_ref[...]
    owner = jnp.zeros_like(atoms)
    for k in range(owner_ref.shape[1]):
        owner = jnp.where(atoms // SUB == k, owner_ref[0, k], owner)
    edge = lax.broadcasted_iota(jnp.int32, atoms.shape, 1)
    place[...] = jnp.where(edge < count_ref[0, 0], owner, -1)
    row = lax.broadcasted_iota(jnp.int32, (SUB, edges), 0)
    match[...] = jnp.where(row == atoms % SUB, 1.0, 0.0).astype(BF16)

    def tell(t, carry):
        some = pl.ds(pl.multiple_of(t * 512, 512), 512)
        hidden = joined_ref[some, :]
        for index in range(w_ref.shape[0]):
            hidden = layer(hidden, w_ref[index])
        message[some, :] = jnp.dot(
            hidden, w_out_ref[...], preferred_element_type=F32
        ).astype(BF16)
        return carry

    lax.fori_loop(0, edges // 512, tell, 0)
    pl.semaphore_wait(barrier, 5)

    def copy(out, into, send, recv, index, device):
        return pltpu.make_async_remote_copy(
            src_ref=out.at[index], dst_ref=into.at[index],
            send_sem=send.at[index], recv_sem=recv.at[index],
            device_id=device, device_id_type=MESH,
        )

    def pair_copy(hop):
        return copy(pair_out, pair_in, pair_send, pair_recv, hop, other)

    def left_y(dy, dx):
        return copy(
            left_y_out, left_y_in, left_y_send, left_y_recv, 2 * (dy - 1) + dx, along_y(dy)
        )

    def left_x():
        return copy(left_x_out, left_x_in, left_x_send, left_x_recv, 0, across)

    def right_x(dy):
        return copy(right_x_out, right_x_in, right_x_send, right_x_recv, dy, across)

    def right_y(dy):
        return copy(right_y_out, right_y_in, right_y_send, right_y_recv, dy - 1, along_y(dy))

    def compute(hop):
        dy, dx = HOPS[hop]
        position = 4 * lax.rem(y + dy, 4) + 2 * lax.rem(xh + dx, 2)

        def chosen(at):
            return match[...] * jnp.where(place[...] == at, 1.0, 0.0).astype(BF16)

        select = jnp.concatenate([chosen(position + 1 - c), chosen(position + c)], axis=0)
        sums = jnp.dot(select, message[...], preferred_element_type=F32)
        pair_out[hop] = sums[:SUB].astype(BF16)
        pair_copy(hop).start()
        mine[hop % 2] = sums[SUB:]

    def pass_on(hop):
        dy, dx = HOPS[hop]
        pair_copy(hop).wait_recv()
        chip_sum = mine[hop % 2] + pair_in[hop].astype(F32)
        if dy:
            left_y_out[2 * (dy - 1) + dx] = chip_sum[:, :half].astype(BF16)
            left_y(dy, dx).start()
        else:
            left_keep[dx] = chip_sum[:, :half]
        if dx:
            right_x_out[dy] = chip_sum[:, half:].astype(BF16)
            right_x(dy).start()
        else:
            right_keep[dy] = chip_sum[:, half:]

    compute(0)
    for hop in range(1, 8):
        compute(hop)
        pass_on(hop - 1)
    pass_on(7)

    for dy in (2, 1, 3):
        right_x(dy).wait_recv()
        right_y_out[dy - 1] = (right_keep[dy] + right_x_in[dy].astype(F32)).astype(BF16)
        right_y(dy).start()

    def gathered(dx):
        value = left_keep[dx]
        for dy in (2, 1, 3):
            left_y(dy, dx).wait_recv()
            value = value + left_y_in[2 * (dy - 1) + dx].astype(F32)
        return value

    left_x_out[0] = gathered(1).astype(BF16)
    left_x().start()
    left_sum = gathered(0)
    right_x(0).wait_recv()
    right_sum = right_keep[0] + right_x_in[0].astype(F32)
    for dy in (1, 3, 2):
        right_y(dy).wait_recv()
        right_sum = right_sum + right_y_in[dy - 1].astype(F32)
    out_ref[:, half:] = right_sum.astype(BF16)
    left_x().wait_recv()
    out_ref[:, :half] = (left_sum + left_x_in[0].astype(F32)).astype(BF16)

    for hop in range(8):
        pair_copy(hop).wait_send()
    left_x().wait_send()
    for dy in range(4):
        right_x(dy).wait_send()
    for dy in (1, 2, 3):
        right_y(dy).wait_send()
        for dx in (0, 1):
            left_y(dy, dx).wait_send()


def owner_sums(joined, w_post, w_out, atoms, count, owners):
    edges, width = joined.shape[0], w_out.shape[1]
    whole = lambda n, kind=BF16: pltpu.VMEM((n, SUB, width), kind)
    halves = lambda n, kind=BF16: pltpu.VMEM((n, SUB, width // 2), kind)
    sems = lambda n: pltpu.SemaphoreType.DMA((n,))
    vmem = pl.BlockSpec(memory_space=pltpu.VMEM)
    smem = pl.BlockSpec(memory_space=pltpu.SMEM)
    return pl.pallas_call(
        owner_kernel,
        name="owner_sums",
        out_shape=jax.ShapeDtypeStruct((SUB, width), BF16),
        in_specs=[vmem, vmem, vmem, vmem, smem, smem],
        out_specs=vmem,
        scratch_shapes=[
            pltpu.VMEM((edges, width), BF16),
            pltpu.VMEM((SUB, edges), BF16),
            pltpu.VMEM(atoms.shape, jnp.int32),
            whole(8), whole(8), whole(2, F32),
            halves(6), halves(6), halves(1), halves(1), halves(2, F32),
            halves(4), halves(4), halves(3), halves(3), halves(4, F32),
            sems(8), sems(8), sems(6), sems(6), sems(1), sems(1),
            sems(4), sems(4), sems(3), sems(3),
        ],
        compiler_params=pltpu.CompilerParams(
            collective_id=1, has_side_effects=True, vmem_limit_bytes=32 << 20
        ),
    )(joined, w_post, w_out, atoms, count, owners)


def shards(edge_feat, tile_counts, reverse_rows, incidence, owner_map, w_pre, w_post, w_out):
    joined = mirror(edge_feat[0, 0], w_pre, reverse_rows[0])
    sums = owner_sums(joined, w_post, w_out, incidence[0], tile_counts, owner_map)
    return sums[None]


def solution(mesh):
    finer = Mesh(mesh.devices.reshape(4, 2, 2, 8, 2), ("y", "xh", "c", "z", "xl"))
    return jax.shard_map(
        shards,
        mesh=finer,
        in_specs=(
            P(SRC, TGT, None, None),
            P(SRC, TGT),
            P(SRC, TGT, None),
            P(SRC, TGT, None),
            P(TGT, None),
            P(),
            P(),
            P(),
        ),
        out_specs=P(TGT, SRC, None),
        check_vma=False,
    )
```

```python
import jax
import jax.numpy as jnp
from jax import lax
from jax.experimental import pallas as pl
from jax.experimental.pallas import tpu as pltpu
from jax.sharding import Mesh
from jax.sharding import PartitionSpec as P

SUB = 256
HALF_ROOT = 0.7071067811865476
MESH = pl.DeviceIdType.MESH
SRC = ("y", "xh", "c")
TGT = ("z", "xl")
CHUNKS = 8
LAGS = (2, 3, 3, 2)
F32 = jnp.float32
BF16 = jnp.bfloat16


def layer(hidden, weight):
    half = jnp.dot(hidden, weight, preferred_element_type=F32) * 0.5
    silu = half + half * jnp.tanh(half)
    return ((hidden.astype(F32) + silu) * HALF_ROOT).astype(BF16)


def where_am_i():
    return tuple(lax.axis_index(name) for name in ("y", "xh", "c", "z", "xl"))


def mirror_kernel(
    edge_ref, w_ref, rev_ref, joined_ref,
    first, spread, midway, moved, landed, detour, total, rev_wide,
    send1, recv1, send2, recv2, send3, recv3, send4, recv4, recv5, send6,
):
    y, xh, c, z, xl = where_am_i()
    zy, z0 = z // 2, lax.rem(z, 2)
    odd = lax.rem(xh + z0, 2)
    relay = odd == 0
    settled = c == xl
    alone = relay & settled
    far = jnp.logical_not(alone)
    leaf = jnp.logical_not(relay)
    rows, width = edge_ref.shape
    chunk = rows // CHUNKS
    piece = chunk // 4

    def along_y(step):
        return (lax.rem(y + step, 4), xh, c, z, xl)

    def along_z(step):
        return (y, xh, c, lax.rem(z + step, 8), xl)

    def along_x(flip):
        return (y, lax.rem(xh + flip, 2), xl, z, c)

    def greet(device):
        pl.semaphore_signal(barrier, inc=1, device_id=device, device_id_type=MESH)

    barrier = pltpu.get_barrier_semaphore()
    for step in range(1, 4):
        greet(along_y(step))
    for step in range(1, 8):
        greet(along_z(step))
    greet(along_x(1))

    @pl.when(jnp.logical_not(settled))
    def _():
        greet(along_x(0))

    def remote(src, dst, send, recv, device):
        return pltpu.make_async_remote_copy(
            src_ref=src, dst_ref=dst, send_sem=send, recv_sem=recv,
            device_id=device, device_id_type=MESH,
        )

    def when(condition, work):
        if condition is True:
            work()
        else:
            pl.when(condition)(work)

    def copy1(g, step):
        start = pl.multiple_of(g * chunk + lax.rem(y + step, 4) * piece, piece)
        return remote(
            first.at[pl.ds(start, piece)], spread.at[g, step],
            send1.at[g, step], recv1.at[g, step], along_y(step),
        )

    def hop2(m):
        return 2 * m + odd

    def held2(m):
        return lax.rem(y + 8 - lax.rem(z + hop2(m), 8) // 2, 4)

    def copy2(x_first, g, m):
        return remote(
            spread.at[g, held2(m)], midway.at[g, hop2(m)],
            send2.at[g, m], recv2.at[g, hop2(m)],
            along_x(odd) if x_first else along_z(hop2(m)),
        )

    def far2(x_first, m):
        return far if x_first else (leaf if m in (0, 2) else True)

    def near2(x_first, m):
        return alone if x_first else (relay if m == 0 else False)

    def slot3(x_first, hop):
        turn = z0 if x_first else 1 - z0
        return lax.rem((hop + (hop % 2) * turn) // 2, 4)

    def copy3(x_first, g, hop):
        return remote(
            midway.at[g, hop], moved.at[g, slot3(x_first, hop)],
            send3.at[g, hop], recv3.at[g, slot3(x_first, hop)],
            along_z(hop) if x_first else along_x(hop % 2),
        )

    def far3(x_first, hop):
        if x_first:
            return relay if hop % 4 else False
        return relay if hop % 2 else relay & far

    def near3(x_first, hop):
        if x_first:
            return False if hop else relay
        return False if hop % 2 else alone

    def got2(g, hop):
        return remote(
            spread.at[g, 0], midway.at[g, hop], send2.at[g, 0], recv2.at[g, hop], along_y(1)
        )

    def got3(g, slot):
        return remote(
            midway.at[g, 0], moved.at[g, slot], send3.at[g, 0], recv3.at[g, slot], along_y(1)
        )

    def detour_out(x_first, g):
        return remote(
            midway.at[g, 4] if x_first else spread.at[g, held2(2)], detour.at[g],
            send3.at[g, 4] if x_first else send2.at[g, 2], recv5.at[g], along_z(2 + 4 * c),
        )

    def detour_on(x_first, g):
        return remote(
            detour.at[g], moved.at[g, 2] if x_first else midway.at[g, 4],
            send6.at[g], recv3.at[g, 2] if x_first else recv2.at[g, 4], along_z(2 + 4 * c),
        )

    def detour_leg(x_first, g):
        @pl.when(relay)
        def _():
            detour_out(x_first, g).wait_recv()
            detour_on(x_first, g).start()

    def copy4(g, step):
        held = lax.rem(zy - y - step + 8, 4)
        return remote(
            moved.at[g, held], landed.at[g, step],
            send4.at[g, step], recv4.at[g, step], along_y(step),
        )

    def embed(g):
        here = pl.ds(pl.multiple_of(g * chunk, chunk), chunk)
        hidden = edge_ref[here, :]
        for index in range(w_ref.shape[0]):
            hidden = layer(hidden, w_ref[index])
        first[here, :] = hidden

    def second_leg(x_first, g):
        for step in range(1, 4):
            copy1(g, step).wait_recv()
        for m in range(4):
            if far2(x_first, m) is not False:
                when(far2(x_first, m), lambda: copy2(x_first, g, m).start())
            if near2(x_first, m) is not False:

                def keep():
                    midway[g, hop2(m)] = spread[g, held2(m)]

                when(near2(x_first, m), keep)
            if m == 2 and not x_first:
                when(relay, lambda: detour_out(False, g).start())

    def third_leg(x_first, g):
        def arrive():
            for hop in range(8):
                if x_first:
                    when(True if hop % 2 else far, lambda: got2(g, hop).wait_recv())
                elif hop:
                    got2(g, hop).wait_recv()

        when(relay, arrive)
        for hop in (4, 3, 5, 2, 6, 1, 7, 0):
            if far3(x_first, hop) is not False:
                when(far3(x_first, hop), lambda: copy3(x_first, g, hop).start())
            if near3(x_first, hop) is not False:

                def keep():
                    moved[g, slot3(x_first, hop)] = midway[g, hop]

                when(near3(x_first, hop), keep)
            if hop == 4 and x_first:
                when(relay, lambda: detour_out(True, g).start())

    def fourth_leg(x_first, g):
        for slot in range(4):
            if x_first:
                when(True if slot else leaf, lambda: got3(g, slot).wait_recv())
            else:
                when(far, lambda: got3(g, slot).wait_recv())

    def by_kind(work, g):
        @pl.when(lax.rem(g, 2) == 0)
        def _():
            work(False, g)

        @pl.when(lax.rem(g, 2) == 1)
        def _():
            work(True, g)

    def stage(i, carry):
        @pl.when(i < CHUNKS)
        def _():
            for step in range(1, 4):
                copy1(i, step).start()
            own = pl.ds(pl.multiple_of(i * chunk + y * piece, piece), piece)
            spread[i, 0] = first[own, :]

        @pl.when(i + 1 < CHUNKS)
        def _():
            embed(i + 1)

        def run(g, leg, kinds=(False, True)):
            for x_first in kinds:

                @pl.when((g >= 0) & (g < CHUNKS) & (lax.rem(g + 2, 2) == int(x_first)))
                def _():
                    leg(x_first, g)

        run(i - LAGS[0], second_leg)
        run(i - LAGS[0] - 1, detour_leg, (False,))
        run(i - sum(LAGS[:2]), third_leg)
        run(i - sum(LAGS[:2]) - 1, detour_leg, (True,))

        @pl.when(i == 2)
        def _():
            total[...] = jnp.zeros_like(total)

        g = i - sum(LAGS[:3])

        @pl.when((g >= 0) & (g < CHUNKS))
        def _():
            by_kind(fourth_leg, g)
            for step in range(1, 4):
                copy4(g, step).start()
            landed[g, 0] = moved[g, lax.rem(zy - y + 4, 4)]

        @pl.when(i >= sum(LAGS))
        def _():
            g = i - sum(LAGS)
            for step in range(1, 4):
                copy4(g, step).wait_recv()
            block = landed[g].reshape(chunk, width)
            lane = lax.broadcasted_iota(jnp.int32, (1, chunk), 1)
            slot, offset = lane // piece, lane % piece
            origin = g * chunk + ((y + 4 - slot) % 4) * piece + offset

            def add(t, carry):
                some = pl.ds(pl.multiple_of(t * 256, 256), 256)
                picked = jnp.concatenate([rev_wide[some, :]] * (chunk // 128), axis=1)
                choose = jnp.where(picked == origin, 1.0, 0.0).astype(BF16)
                total[some, :] += jnp.dot(choose, block, preferred_element_type=F32)
                return carry

            lax.fori_loop(0, rows // 256, add, 0)

        return carry

    embed(0)

    def widen(t, carry):
        part = pl.ds(pl.multiple_of(t * 128, 128), 128)
        rev_wide[part, :] = jnp.broadcast_to(rev_ref[:, part], (128, 128)).T
        return carry

    lax.fori_loop(0, rows // 128, widen, 0)
    pl.semaphore_wait(barrier, jnp.where(settled, 11, 12))
    lax.fori_loop(0, CHUNKS + sum(LAGS), stage, 0)

    def sent(x_first, g):
        for m in range(4):
            when(far2(x_first, m), lambda: copy2(x_first, g, m).wait_send())
        for hop in range(8):
            if far3(x_first, hop) is not False:
                when(far3(x_first, hop), lambda: copy3(x_first, g, hop).wait_send())

        @pl.when(relay)
        def _():
            detour_out(x_first, g).wait_send()
            detour_on(x_first, g).wait_send()


    def finish(g, carry):
        here = pl.ds(pl.multiple_of(g * chunk, chunk), chunk)
        both = first[here, :].astype(F32) + total[here, :]
        joined_ref[here, :] = (both * HALF_ROOT).astype(BF16)
        for step in range(1, 4):
            copy1(g, step).wait_send()
            copy4(g, step).wait_send()
        by_kind(sent, g)
        return carry

    lax.fori_loop(0, CHUNKS, finish, 0)


def mirror(edge, w_pre, rev):
    rows, width = edge.shape
    piece = rows // CHUNKS // 4
    pieces = lambda n: pltpu.VMEM((CHUNKS, n, piece, width), BF16)
    sems = lambda n: pltpu.SemaphoreType.DMA((CHUNKS, n))
    vmem = pl.BlockSpec(memory_space=pltpu.VMEM)
    return pl.pallas_call(
        mirror_kernel,
        name="mirror",
        out_shape=jax.ShapeDtypeStruct((rows, width), BF16),
        in_specs=[vmem] * 3,
        out_specs=vmem,
        scratch_shapes=[
            pltpu.VMEM((rows, width), BF16),
            pieces(4), pieces(8), pieces(4), pieces(4),
            pltpu.VMEM((CHUNKS, piece, width), BF16),
            pltpu.VMEM((rows, width), F32),
            pltpu.VMEM((rows, 128), jnp.int32),
            sems(4), sems(4), sems(4), sems(8), sems(8), sems(4), sems(4), sems(4),
            pltpu.SemaphoreType.DMA((CHUNKS,)), pltpu.SemaphoreType.DMA((CHUNKS,)),
        ],
        compiler_params=pltpu.CompilerParams(
            collective_id=0, has_side_effects=True, vmem_limit_bytes=40 << 20
        ),
    )(edge, w_pre, rev)


HOPS = ((2, 1), (1, 1), (3, 1), (0, 1), (2, 0), (1, 0), (3, 0), (0, 0))


def owner_kernel(
    joined_ref, w_ref, w_out_ref, atom_ref, count_ref, owner_ref, out_ref,
    message, match, place, pair_out, pair_in, mine,
    left_y_out, left_y_in, left_x_out, left_x_in, left_keep,
    right_x_out, right_x_in, right_y_out, right_y_in, right_keep,
    pair_send, pair_recv, left_y_send, left_y_recv, left_x_send, left_x_recv,
    right_x_send, right_x_recv, right_y_send, right_y_recv,
):
    y, xh, c, z, xl = where_am_i()
    edges, width = message.shape
    half = width // 2
    other = (y, xh, 1 - c, z, xl)
    across = (y, 1 - xh, c, z, xl)

    def along_y(step):
        return (lax.rem(y + step, 4), xh, c, z, xl)

    barrier = pltpu.get_barrier_semaphore()
    for device in (other, across, along_y(1), along_y(2), along_y(3)):
        pl.semaphore_signal(barrier, inc=1, device_id=device, device_id_type=MESH)

    atoms = atom_ref[...]
    owner = jnp.zeros_like(atoms)
    for k in range(owner_ref.shape[1]):
        owner = jnp.where(atoms // SUB == k, owner_ref[0, k], owner)
    edge = lax.broadcasted_iota(jnp.int32, atoms.shape, 1)
    place[...] = jnp.where(edge < count_ref[0, 0], owner, -1)
    row = lax.broadcasted_iota(jnp.int32, (SUB, edges), 0)
    match[...] = jnp.where(row == atoms % SUB, 1.0, 0.0).astype(BF16)

    def tell(t, carry):
        some = pl.ds(pl.multiple_of(t * 512, 512), 512)
        hidden = joined_ref[some, :]
        for index in range(w_ref.shape[0]):
            hidden = layer(hidden, w_ref[index])
        message[some, :] = jnp.dot(
            hidden, w_out_ref[...], preferred_element_type=F32
        ).astype(BF16)
        return carry

    lax.fori_loop(0, edges // 512, tell, 0)
    pl.semaphore_wait(barrier, 5)

    def copy(out, into, send, recv, index, device):
        return pltpu.make_async_remote_copy(
            src_ref=out.at[index], dst_ref=into.at[index],
            send_sem=send.at[index], recv_sem=recv.at[index],
            device_id=device, device_id_type=MESH,
        )

    def pair_copy(hop):
        return copy(pair_out, pair_in, pair_send, pair_recv, hop, other)

    def left_y(dy, dx):
        return copy(
            left_y_out, left_y_in, left_y_send, left_y_recv, 2 * (dy - 1) + dx, along_y(dy)
        )

    def left_x():
        return copy(left_x_out, left_x_in, left_x_send, left_x_recv, 0, across)

    def right_x(dy):
        return copy(right_x_out, right_x_in, right_x_send, right_x_recv, dy, across)

    def right_y(dy):
        return copy(right_y_out, right_y_in, right_y_send, right_y_recv, dy - 1, along_y(dy))

    def compute(hop):
        dy, dx = HOPS[hop]
        position = 4 * lax.rem(y + dy, 4) + 2 * lax.rem(xh + dx, 2)

        def chosen(at):
            return match[...] * jnp.where(place[...] == at, 1.0, 0.0).astype(BF16)

        select = jnp.concatenate([chosen(position + 1 - c), chosen(position + c)], axis=0)
        sums = jnp.dot(select, message[...], preferred_element_type=F32)
        pair_out[hop] = sums[:SUB].astype(BF16)
        pair_copy(hop).start()
        mine[hop % 2] = sums[SUB:]

    def pass_on(hop):
        dy, dx = HOPS[hop]
        pair_copy(hop).wait_recv()
        chip_sum = mine[hop % 2] + pair_in[hop].astype(F32)
        if dy:
            left_y_out[2 * (dy - 1) + dx] = chip_sum[:, :half].astype(BF16)
            left_y(dy, dx).start()
        else:
            left_keep[dx] = chip_sum[:, :half]
        if dx:
            right_x_out[dy] = chip_sum[:, half:].astype(BF16)
            right_x(dy).start()
        else:
            right_keep[dy] = chip_sum[:, half:]

    compute(0)
    for hop in range(1, 8):
        compute(hop)
        pass_on(hop - 1)
    pass_on(7)

    for dy in (2, 1, 3):
        right_x(dy).wait_recv()
        right_y_out[dy - 1] = (right_keep[dy] + right_x_in[dy].astype(F32)).astype(BF16)
        right_y(dy).start()

    def gathered(dx):
        value = left_keep[dx]
        for dy in (2, 1, 3):
            left_y(dy, dx).wait_recv()
            value = value + left_y_in[2 * (dy - 1) + dx].astype(F32)
        return value

    left_x_out[0] = gathered(1).astype(BF16)
    left_x().start()
    left_sum = gathered(0)
    right_x(0).wait_recv()
    right_sum = right_keep[0] + right_x_in[0].astype(F32)
    for dy in (1, 3, 2):
        right_y(dy).wait_recv()
        right_sum = right_sum + right_y_in[dy - 1].astype(F32)
    out_ref[:, half:] = right_sum.astype(BF16)
    left_x().wait_recv()
    out_ref[:, :half] = (left_sum + left_x_in[0].astype(F32)).astype(BF16)

    for hop in range(8):
        pair_copy(hop).wait_send()
    left_x().wait_send()
    for dy in range(4):
        right_x(dy).wait_send()
    for dy in (1, 2, 3):
        right_y(dy).wait_send()
        for dx in (0, 1):
            left_y(dy, dx).wait_send()


def owner_sums(joined, w_post, w_out, atoms, count, owners):
    edges, width = joined.shape[0], w_out.shape[1]
    whole = lambda n, kind=BF16: pltpu.VMEM((n, SUB, width), kind)
    halves = lambda n, kind=BF16: pltpu.VMEM((n, SUB, width // 2), kind)
    sems = lambda n: pltpu.SemaphoreType.DMA((n,))
    vmem = pl.BlockSpec(memory_space=pltpu.VMEM)
    smem = pl.BlockSpec(memory_space=pltpu.SMEM)
    return pl.pallas_call(
        owner_kernel,
        name="owner_sums",
        out_shape=jax.ShapeDtypeStruct((SUB, width), BF16),
        in_specs=[vmem, vmem, vmem, vmem, smem, smem],
        out_specs=vmem,
        scratch_shapes=[
            pltpu.VMEM((edges, width), BF16),
            pltpu.VMEM((SUB, edges), BF16),
            pltpu.VMEM(atoms.shape, jnp.int32),
            whole(8), whole(8), whole(2, F32),
            halves(6), halves(6), halves(1), halves(1), halves(2, F32),
            halves(4), halves(4), halves(3), halves(3), halves(4, F32),
            sems(8), sems(8), sems(6), sems(6), sems(1), sems(1),
            sems(4), sems(4), sems(3), sems(3),
        ],
        compiler_params=pltpu.CompilerParams(
            collective_id=1, has_side_effects=True, vmem_limit_bytes=32 << 20
        ),
    )(joined, w_post, w_out, atoms, count, owners)


def shards(edge_feat, tile_counts, reverse_rows, incidence, owner_map, w_pre, w_post, w_out):
    joined = mirror(edge_feat[0, 0], w_pre, reverse_rows[0])
    sums = owner_sums(joined, w_post, w_out, incidence[0], tile_counts, owner_map)
    return sums[None]


def solution(mesh):
    finer = Mesh(mesh.devices.reshape(4, 2, 2, 8, 2), ("y", "xh", "c", "z", "xl"))
    return jax.shard_map(
        shards,
        mesh=finer,
        in_specs=(
            P(SRC, TGT, None, None),
            P(SRC, TGT),
            P(SRC, TGT, None),
            P(SRC, TGT, None),
            P(TGT, None),
            P(),
            P(),
            P(),
        ),
        out_specs=P(TGT, SRC, None),
        check_vma=False,
    )
```

```python
import jax
import jax.numpy as jnp
from jax import lax
from jax.experimental import pallas as pl
from jax.experimental.pallas import tpu as pltpu
from jax.sharding import Mesh
from jax.sharding import PartitionSpec as P

SUB = 256
HALF_ROOT = 0.7071067811865476
MESH = pl.DeviceIdType.MESH
SRC = ("y", "xh", "c")
TGT = ("z", "xl")
CHUNKS = 8
LAGS = (2, 3, 3, 2)
VMEM_BYTES = 62 << 20
F32 = jnp.float32
BF16 = jnp.bfloat16


def layer(hidden, weight):
    half = jnp.dot(hidden, weight, preferred_element_type=F32) * 0.5
    silu = half + half * jnp.tanh(half)
    return ((hidden.astype(F32) + silu) * HALF_ROOT).astype(BF16)


def where_am_i():
    return tuple(lax.axis_index(name) for name in ("y", "xh", "c", "z", "xl"))


HOPS = ((2, 1), (1, 1), (3, 1), (0, 1), (2, 0), (1, 0), (3, 0), (0, 0))


def edge_kernel(
    edge_hbm, w_hbm, rev_hbm, w_post_hbm, w_out_hbm, atom_hbm, count_hbm, owner_hbm, out_ref,
    edge_ref, w_ref, rev_ref, w_post_ref, w_out_ref, atom_ref, count_ref, owner_ref, load, first, spread, midway, moved, landed, detour, total, rev_wide,
    send1, recv1, send2, recv2, send3, recv3, send4, recv4, recv5, send6,
    message, match, place, pair_out, pair_in, mine,
    left_y_out, left_y_in, left_x_out, left_x_in, left_keep,
    right_x_out, right_x_in, right_y_out, right_y_in, right_keep,
    pair_send, pair_recv, left_y_send, left_y_recv, left_x_send, left_x_recv,
    right_x_send, right_x_recv, right_y_send, right_y_recv,
):
    y, xh, c, z, xl = where_am_i()
    zy, z0 = z // 2, lax.rem(z, 2)
    odd = lax.rem(xh + z0, 2)
    relay = odd == 0
    settled = c == xl
    alone = relay & settled
    far = jnp.logical_not(alone)
    leaf = jnp.logical_not(relay)
    rows, width = edge_ref.shape
    layers = w_ref.shape[0]
    chunk = rows // CHUNKS
    piece = chunk // 4

    edges, message_width = message.shape
    half = message_width // 2
    other = (y, xh, 1 - c, z, xl)
    across = (y, 1 - xh, c, z, xl)

    def along_y(step):
        return (lax.rem(y + step, 4), xh, c, z, xl)

    def along_z(step):
        return (y, xh, c, lax.rem(z + step, 8), xl)

    def along_x(flip):
        return (y, lax.rem(xh + flip, 2), xl, z, c)

    def greet(device):
        pl.semaphore_signal(barrier, inc=1, device_id=device, device_id_type=MESH)

    barrier = pltpu.get_barrier_semaphore()
    for step in range(1, 4):
        greet(along_y(step))
    for step in range(1, 8):
        greet(along_z(step))
    greet(along_x(1))
    greet(other)

    @pl.when(jnp.logical_not(settled))
    def _():
        greet(along_x(0))
        greet(across)

    head, tail = pl.ds(0, chunk), pl.ds(chunk, rows - chunk)
    load_w = pltpu.make_async_copy(w_hbm, w_ref, load.at[0])
    load_head = pltpu.make_async_copy(edge_hbm.at[head], edge_ref.at[head], load.at[1])
    load_tail = pltpu.make_async_copy(edge_hbm.at[tail], edge_ref.at[tail], load.at[2])
    load_rev = pltpu.make_async_copy(rev_hbm, rev_ref, load.at[3])
    load_rest = [
        pltpu.make_async_copy(out, into, load.at[4 + index])
        for index, (out, into) in enumerate((
            (w_post_hbm, w_post_ref), (w_out_hbm, w_out_ref), (atom_hbm, atom_ref),
            (count_hbm, count_ref), (owner_hbm, owner_ref),
        ))
    ]
    for item in (load_head, load_w, load_rev, load_tail, *load_rest):
        item.start()

    def remote(src, dst, send, recv, device):
        return pltpu.make_async_remote_copy(
            src_ref=src, dst_ref=dst, send_sem=send, recv_sem=recv,
            device_id=device, device_id_type=MESH,
        )

    def when(condition, work):
        if condition is True:
            work()
        else:
            pl.when(condition)(work)

    def copy1(g, step):
        start = pl.multiple_of(g * chunk + lax.rem(y + step, 4) * piece, piece)
        return remote(
            first.at[pl.ds(start, piece)], spread.at[g, step],
            send1.at[g, step], recv1.at[g, step], along_y(step),
        )

    def hop2(m):
        return 2 * m + odd

    def held2(m):
        return lax.rem(y + 8 - lax.rem(z + hop2(m), 8) // 2, 4)

    def copy2(x_first, g, m):
        return remote(
            spread.at[g, held2(m)], midway.at[g, hop2(m)],
            send2.at[g, m], recv2.at[g, hop2(m)],
            along_x(odd) if x_first else along_z(hop2(m)),
        )

    def far2(x_first, m):
        return far if x_first else (leaf if m in (0, 2) else True)

    def near2(x_first, m):
        return alone if x_first else (relay if m == 0 else False)

    def slot3(x_first, hop):
        turn = z0 if x_first else 1 - z0
        return lax.rem((hop + (hop % 2) * turn) // 2, 4)

    def copy3(x_first, g, hop):
        return remote(
            midway.at[g, hop], moved.at[g, slot3(x_first, hop)],
            send3.at[g, hop], recv3.at[g, slot3(x_first, hop)],
            along_z(hop) if x_first else along_x(hop % 2),
        )

    def far3(x_first, hop):
        if x_first:
            return relay if hop % 4 else False
        return relay if hop % 2 else relay & far

    def near3(x_first, hop):
        if x_first:
            return False if hop else relay
        return False if hop % 2 else alone

    def got2(g, hop):
        return remote(
            spread.at[g, 0], midway.at[g, hop], send2.at[g, 0], recv2.at[g, hop], along_y(1)
        )

    def got3(g, slot):
        return remote(
            midway.at[g, 0], moved.at[g, slot], send3.at[g, 0], recv3.at[g, slot], along_y(1)
        )

    def detour_out(x_first, g):
        return remote(
            midway.at[g, 4] if x_first else spread.at[g, held2(2)], detour.at[g],
            send3.at[g, 4] if x_first else send2.at[g, 2], recv5.at[g], along_z(2 + 4 * c),
        )

    def detour_on(x_first, g):
        return remote(
            detour.at[g], moved.at[g, 2] if x_first else midway.at[g, 4],
            send6.at[g], recv3.at[g, 2] if x_first else recv2.at[g, 4], along_z(2 + 4 * c),
        )

    def detour_leg(x_first, g):
        @pl.when(relay)
        def _():
            detour_out(x_first, g).wait_recv()
            detour_on(x_first, g).start()

    def copy4(g, step):
        held = lax.rem(zy - y - step + 8, 4)
        return remote(
            moved.at[g, held], landed.at[g, step],
            send4.at[g, step], recv4.at[g, step], along_y(step),
        )

    def embed(g):
        here = pl.ds(pl.multiple_of(g * chunk, chunk), chunk)
        hidden = edge_ref[here, :]
        for index in range(layers):
            hidden = layer(hidden, w_ref[index])
        first[here, :] = hidden

    def second_leg(x_first, g):
        for step in range(1, 4):
            copy1(g, step).wait_recv()
        for m in range(4):
            if far2(x_first, m) is not False:
                when(far2(x_first, m), lambda: copy2(x_first, g, m).start())
            if near2(x_first, m) is not False:

                def keep():
                    midway[g, hop2(m)] = spread[g, held2(m)]

                when(near2(x_first, m), keep)
            if m == 2 and not x_first:
                when(relay, lambda: detour_out(False, g).start())

    def third_leg(x_first, g):
        def arrive():
            for hop in range(8):
                if x_first:
                    when(True if hop % 2 else far, lambda: got2(g, hop).wait_recv())
                elif hop:
                    got2(g, hop).wait_recv()

        when(relay, arrive)
        for hop in (4, 3, 5, 2, 6, 1, 7, 0):
            if far3(x_first, hop) is not False:
                when(far3(x_first, hop), lambda: copy3(x_first, g, hop).start())
            if near3(x_first, hop) is not False:

                def keep():
                    moved[g, slot3(x_first, hop)] = midway[g, hop]

                when(near3(x_first, hop), keep)
            if hop == 4 and x_first:
                when(relay, lambda: detour_out(True, g).start())

    def fourth_leg(x_first, g):
        for slot in range(4):
            if x_first:
                when(True if slot else leaf, lambda: got3(g, slot).wait_recv())
            else:
                when(far, lambda: got3(g, slot).wait_recv())

    def sent(x_first, g):
        for m in range(4):
            when(far2(x_first, m), lambda: copy2(x_first, g, m).wait_send())
        for hop in range(8):
            if far3(x_first, hop) is not False:
                when(far3(x_first, hop), lambda: copy3(x_first, g, hop).wait_send())

        @pl.when(relay)
        def _():
            detour_out(x_first, g).wait_send()
            detour_on(x_first, g).wait_send()


    def by_kind(work, g):
        @pl.when(lax.rem(g, 2) == 0)
        def _():
            work(False, g)

        @pl.when(lax.rem(g, 2) == 1)
        def _():
            work(True, g)

    def stage(i, carry):
        @pl.when(i < CHUNKS)
        def _():
            for step in range(1, 4):
                copy1(i, step).start()
            own = pl.ds(pl.multiple_of(i * chunk + y * piece, piece), piece)
            spread[i, 0] = first[own, :]

        @pl.when(i + 1 < CHUNKS)
        def _():
            embed(i + 1)

        def run(g, leg, kinds=(False, True)):
            for x_first in kinds:

                @pl.when((g >= 0) & (g < CHUNKS) & (lax.rem(g + 2, 2) == int(x_first)))
                def _():
                    leg(x_first, g)

        run(i - LAGS[0], second_leg)
        run(i - LAGS[0] - 1, detour_leg, (False,))
        run(i - sum(LAGS[:2]), third_leg)
        run(i - sum(LAGS[:2]) - 1, detour_leg, (True,))

        @pl.when(i == 2)
        def _():
            total[...] = jnp.zeros_like(total)
            for item in load_rest:
                item.wait()
            atoms = atom_ref[...]
            owner = jnp.zeros_like(atoms)
            for k in range(owner_ref.shape[1]):
                owner = jnp.where(atoms // SUB == k, owner_ref[:, k : k + 1], owner)
            edge = lax.broadcasted_iota(jnp.int32, atoms.shape, 1)
            place[...] = jnp.where(edge < count_ref[...], owner, -1)
            row = lax.broadcasted_iota(jnp.int32, (SUB, edges), 0)
            match[...] = jnp.where(row == atoms % SUB, 1.0, 0.0).astype(BF16)

        g = i - sum(LAGS[:3])

        @pl.when((g >= 0) & (g < CHUNKS))
        def _():
            by_kind(fourth_leg, g)
            for step in range(1, 4):
                copy4(g, step).start()
            landed[g, 0] = moved[g, lax.rem(zy - y + 4, 4)]

        @pl.when(i >= sum(LAGS))
        def _():
            g = i - sum(LAGS)
            for step in range(1, 4):
                copy4(g, step).wait_recv()
            block = landed[g].reshape(chunk, width)
            lane = lax.broadcasted_iota(jnp.int32, (1, chunk), 1)
            slot, offset = lane // piece, lane % piece
            origin = g * chunk + ((y + 4 - slot) % 4) * piece + offset

            def picked(some):
                wide = jnp.concatenate([rev_wide[some, :]] * (chunk // 128), axis=1)
                choose = jnp.where(wide == origin, 1.0, 0.0).astype(BF16)
                return total[some, :] + jnp.dot(choose, block, preferred_element_type=F32)

            def add(t, carry):
                some = pl.ds(pl.multiple_of(t * 256, 256), 256)
                total[some, :] = picked(some)
                return carry

            def tell(t, carry):
                some = pl.ds(pl.multiple_of(t * 256, 256), 256)
                both = first[some, :].astype(F32) + picked(some)
                hidden = (both * HALF_ROOT).astype(BF16)
                for index in range(layers):
                    hidden = layer(hidden, w_post_ref[index])
                message[some, :] = jnp.dot(
                    hidden, w_out_ref[...], preferred_element_type=F32
                ).astype(BF16)
                return carry

            @pl.when(g < CHUNKS - 1)
            def _():
                lax.fori_loop(0, rows // 256, add, 0)

            @pl.when(g == CHUNKS - 1)
            def _():
                lax.fori_loop(0, rows // 256, tell, 0)

            for step in range(1, 4):
                copy1(g, step).wait_send()
                copy4(g, step).wait_send()
            by_kind(sent, g)

        return carry

    load_head.wait()
    load_w.wait()
    embed(0)
    load_rev.wait()

    def widen(t, carry):
        part = pl.ds(pl.multiple_of(t * 128, 128), 128)
        rev_wide[part, :] = jnp.broadcast_to(rev_ref[:, part], (128, 128)).T
        return carry

    lax.fori_loop(0, rows // 128, widen, 0)
    load_tail.wait()
    pl.semaphore_wait(barrier, jnp.where(settled, 12, 14))
    lax.fori_loop(0, CHUNKS + sum(LAGS), stage, 0)

    def owner_copy(out, into, send, recv, index, device):
        return pltpu.make_async_remote_copy(
            src_ref=out.at[index], dst_ref=into.at[index],
            send_sem=send.at[index], recv_sem=recv.at[index],
            device_id=device, device_id_type=MESH,
        )

    def pair_copy(hop):
        return owner_copy(pair_out, pair_in, pair_send, pair_recv, hop, other)

    def left_y(dy, dx):
        return owner_copy(
            left_y_out, left_y_in, left_y_send, left_y_recv, 2 * (dy - 1) + dx, along_y(dy)
        )

    def left_x():
        return owner_copy(left_x_out, left_x_in, left_x_send, left_x_recv, 0, across)

    def right_x(dy):
        return owner_copy(right_x_out, right_x_in, right_x_send, right_x_recv, dy, across)

    def right_y(dy):
        return owner_copy(right_y_out, right_y_in, right_y_send, right_y_recv, dy - 1, along_y(dy))

    def compute(hop):
        dy, dx = HOPS[hop]
        position = 4 * lax.rem(y + dy, 4) + 2 * lax.rem(xh + dx, 2)

        def chosen(at):
            return match[...] * jnp.where(place[...] == at, 1.0, 0.0).astype(BF16)

        select = jnp.concatenate([chosen(position + 1 - c), chosen(position + c)], axis=0)
        sums = jnp.dot(select, message[...], preferred_element_type=F32)
        pair_out[hop] = sums[:SUB].astype(BF16)
        pair_copy(hop).start()
        mine[hop % 2] = sums[SUB:]

    def pass_on(hop):
        dy, dx = HOPS[hop]
        pair_copy(hop).wait_recv()
        chip_sum = mine[hop % 2] + pair_in[hop].astype(F32)
        if dy:
            left_y_out[2 * (dy - 1) + dx] = chip_sum[:, :half].astype(BF16)
            left_y(dy, dx).start()
        else:
            left_keep[dx] = chip_sum[:, :half]
        if dx:
            right_x_out[dy] = chip_sum[:, half:].astype(BF16)
            right_x(dy).start()
        else:
            right_keep[dy] = chip_sum[:, half:]

    compute(0)
    for hop in range(1, 8):
        compute(hop)
        pass_on(hop - 1)
    pass_on(7)

    for dy in (2, 1, 3):
        right_x(dy).wait_recv()
        right_y_out[dy - 1] = (right_keep[dy] + right_x_in[dy].astype(F32)).astype(BF16)
        right_y(dy).start()

    def gathered(dx):
        value = left_keep[dx]
        for dy in (2, 1, 3):
            left_y(dy, dx).wait_recv()
            value = value + left_y_in[2 * (dy - 1) + dx].astype(F32)
        return value

    left_x_out[0] = gathered(1).astype(BF16)
    left_x().start()
    left_sum = gathered(0)
    right_x(0).wait_recv()
    right_sum = right_keep[0] + right_x_in[0].astype(F32)
    for dy in (1, 3, 2):
        right_y(dy).wait_recv()
        right_sum = right_sum + right_y_in[dy - 1].astype(F32)
    out_ref[:, half:] = right_sum.astype(BF16)
    left_x().wait_recv()
    out_ref[:, :half] = (left_sum + left_x_in[0].astype(F32)).astype(BF16)

    for hop in range(8):
        pair_copy(hop).wait_send()
    left_x().wait_send()
    for dy in range(4):
        right_x(dy).wait_send()
    for dy in (1, 2, 3):
        right_y(dy).wait_send()
        for dx in (0, 1):
            left_y(dy, dx).wait_send()


def edge_block(*operands):
    edge, w_pre, rev, w_post, w_out, atoms, count, owners = operands
    rows, width = edge.shape
    message_width = w_out.shape[1]
    piece = rows // CHUNKS // 4
    pieces = lambda n: pltpu.VMEM((CHUNKS, n, piece, width), BF16)
    grid_sems = lambda n: pltpu.SemaphoreType.DMA((CHUNKS, n))
    whole = lambda n, kind=BF16: pltpu.VMEM((n, SUB, message_width), kind)
    halves = lambda n, kind=BF16: pltpu.VMEM((n, SUB, message_width // 2), kind)
    sems = lambda n: pltpu.SemaphoreType.DMA((n,))
    return pl.pallas_call(
        edge_kernel,
        name="edge_block",
        out_shape=jax.ShapeDtypeStruct((SUB, message_width), BF16),
        in_specs=[pl.BlockSpec(memory_space=pltpu.HBM)] * len(operands),
        out_specs=pl.BlockSpec(memory_space=pltpu.VMEM),
        scratch_shapes=[
            *(pltpu.VMEM(operand.shape, operand.dtype) for operand in operands),
            sems(9),
            pltpu.VMEM((rows, width), BF16),
            pieces(4), pieces(8), pieces(4), pieces(4),
            pltpu.VMEM((CHUNKS, piece, width), BF16),
            pltpu.VMEM((rows, width), F32),
            pltpu.VMEM((rows, 128), jnp.int32),
            *(grid_sems(n) for n in (4, 4, 4, 8, 8, 4, 4, 4)),
            sems(CHUNKS), sems(CHUNKS),
            pltpu.VMEM((rows, message_width), BF16),
            pltpu.VMEM((SUB, rows), BF16),
            pltpu.VMEM(atoms.shape, jnp.int32),
            whole(8), whole(8), whole(2, F32),
            halves(6), halves(6), halves(1), halves(1), halves(2, F32),
            halves(4), halves(4), halves(3), halves(3), halves(4, F32),
            *(sems(n) for n in (8, 8, 6, 6, 1, 1, 4, 4, 3, 3)),
        ],
        compiler_params=pltpu.CompilerParams(
            collective_id=0, has_side_effects=True, vmem_limit_bytes=VMEM_BYTES
        ),
    )(*operands)


def shards(edge_feat, tile_counts, reverse_rows, incidence, owner_map, w_pre, w_post, w_out):
    return edge_block(
        edge_feat[0, 0], w_pre, reverse_rows[0], w_post, w_out,
        incidence[0], tile_counts, owner_map,
    )[None]


def solution(mesh):
    finer = Mesh(mesh.devices.reshape(4, 2, 2, 8, 2), ("y", "xh", "c", "z", "xl"))
    return jax.shard_map(
        shards,
        mesh=finer,
        in_specs=(
            P(SRC, TGT, None, None),
            P(SRC, TGT),
            P(SRC, TGT, None),
            P(SRC, TGT, None),
            P(TGT, None),
            P(),
            P(),
            P(),
        ),
        out_specs=P(TGT, SRC, None),
        check_vma=False,
    )
```

```python
import jax
import jax.numpy as jnp
from jax import lax
from jax.experimental import pallas as pl
from jax.experimental.pallas import tpu as pltpu
from jax.sharding import Mesh
from jax.sharding import PartitionSpec as P

SUB = 256
HALF_ROOT = 0.7071067811865476
MESH = pl.DeviceIdType.MESH
SRC = ("y", "xh", "c")
TGT = ("z", "xl")
CHUNKS = 8
LAGS = (2, 3, 3, 2)
VMEM_BYTES = 62 << 20
F32 = jnp.float32
BF16 = jnp.bfloat16


def layer(hidden, weight):
    half = jnp.dot(hidden, weight, preferred_element_type=F32) * 0.5
    silu = half + half * jnp.tanh(half)
    return ((hidden.astype(F32) + silu) * HALF_ROOT).astype(BF16)


def where_am_i():
    return tuple(lax.axis_index(name) for name in ("y", "xh", "c", "z", "xl"))


HOPS = ((2, 1), (1, 1), (3, 1), (0, 1), (2, 0), (1, 0), (3, 0), (0, 0))


def edge_kernel(
    edge_hbm, w_hbm, rev_hbm, w_post_hbm, w_out_hbm, atom_hbm, count_hbm, owner_hbm, out_ref,
    edge_ref, w_ref, rev_ref, w_post_ref, w_out_ref, atom_ref, count_ref, owner_ref, load, first, spread, midway, moved, landed, detour, total, rev_wide,
    send1, recv1, send2, recv2, send3, recv3, send4, recv4, recv5, send6,
    message, match, place, pair_out, pair_in, mine,
    left_y_out, left_y_in, left_x_out, left_x_in, left_keep,
    right_x_out, right_x_in, right_y_out, right_y_in, right_keep,
    pair_send, pair_recv, left_y_send, left_y_recv, left_x_send, left_x_recv,
    right_x_send, right_x_recv, right_y_send, right_y_recv,
):
    y, xh, c, z, xl = where_am_i()
    zy, z0 = z // 2, lax.rem(z, 2)
    odd = lax.rem(xh + z0, 2)
    relay = odd == 0
    settled = c == xl
    alone = relay & settled
    far = jnp.logical_not(alone)
    leaf = jnp.logical_not(relay)
    rows, width = edge_ref.shape
    layers = w_ref.shape[0]
    chunk = rows // CHUNKS
    piece = chunk // 4

    edges, message_width = message.shape
    half = message_width // 2
    other = (y, xh, 1 - c, z, xl)
    across = (y, 1 - xh, c, z, xl)

    def along_y(step):
        return (lax.rem(y + step, 4), xh, c, z, xl)

    def along_z(step):
        return (y, xh, c, lax.rem(z + step, 8), xl)

    def along_x(flip):
        return (y, lax.rem(xh + flip, 2), xl, z, c)

    def greet(device):
        pl.semaphore_signal(barrier, inc=1, device_id=device, device_id_type=MESH)

    barrier = pltpu.get_barrier_semaphore()
    for step in range(1, 4):
        greet(along_y(step))
    for step in range(1, 8):
        greet(along_z(step))
    greet(along_x(1))
    greet(other)

    @pl.when(jnp.logical_not(settled))
    def _():
        greet(along_x(0))
        greet(across)

    head, tail = pl.ds(0, chunk), pl.ds(chunk, rows - chunk)
    load_w = pltpu.make_async_copy(w_hbm, w_ref, load.at[0])
    load_head = pltpu.make_async_copy(edge_hbm.at[head], edge_ref.at[head], load.at[1])
    load_tail = pltpu.make_async_copy(edge_hbm.at[tail], edge_ref.at[tail], load.at[2])
    load_rev = pltpu.make_async_copy(rev_hbm, rev_ref, load.at[3])
    load_rest = [
        pltpu.make_async_copy(out, into, load.at[4 + index])
        for index, (out, into) in enumerate((
            (w_post_hbm, w_post_ref), (w_out_hbm, w_out_ref), (atom_hbm, atom_ref),
            (count_hbm, count_ref), (owner_hbm, owner_ref),
        ))
    ]
    for item in (load_head, load_w, load_rev):
        item.start()

    def remote(src, dst, send, recv, device):
        return pltpu.make_async_remote_copy(
            src_ref=src, dst_ref=dst, send_sem=send, recv_sem=recv,
            device_id=device, device_id_type=MESH,
        )

    def when(condition, work):
        if condition is True:
            work()
        else:
            pl.when(condition)(work)

    def copy1(g, step):
        start = pl.multiple_of(g * chunk + lax.rem(y + step, 4) * piece, piece)
        return remote(
            first.at[pl.ds(start, piece)], spread.at[g, step],
            send1.at[g, step], recv1.at[g, step], along_y(step),
        )

    def hop2(m):
        return 2 * m + odd

    def held2(m):
        return lax.rem(y + 8 - lax.rem(z + hop2(m), 8) // 2, 4)

    def copy2(x_first, g, m):
        return remote(
            spread.at[g, held2(m)], midway.at[g, hop2(m)],
            send2.at[g, m], recv2.at[g, hop2(m)],
            along_x(odd) if x_first else along_z(hop2(m)),
        )

    def far2(x_first, m):
        return far if x_first else (leaf if m in (0, 2) else True)

    def near2(x_first, m):
        return alone if x_first else (relay if m == 0 else False)

    def slot3(x_first, hop):
        turn = z0 if x_first else 1 - z0
        return lax.rem((hop + (hop % 2) * turn) // 2, 4)

    def copy3(x_first, g, hop):
        return remote(
            midway.at[g, hop], moved.at[g, slot3(x_first, hop)],
            send3.at[g, hop], recv3.at[g, slot3(x_first, hop)],
            along_z(hop) if x_first else along_x(hop % 2),
        )

    def far3(x_first, hop):
        if x_first:
            return relay if hop % 4 else False
        return relay if hop % 2 else relay & far

    def near3(x_first, hop):
        if x_first:
            return False if hop else relay
        return False if hop % 2 else alone

    def got2(g, hop):
        return remote(
            spread.at[g, 0], midway.at[g, hop], send2.at[g, 0], recv2.at[g, hop], along_y(1)
        )

    def got3(g, slot):
        return remote(
            midway.at[g, 0], moved.at[g, slot], send3.at[g, 0], recv3.at[g, slot], along_y(1)
        )

    def detour_out(x_first, g):
        return remote(
            midway.at[g, 4] if x_first else spread.at[g, held2(2)], detour.at[g],
            send3.at[g, 4] if x_first else send2.at[g, 2], recv5.at[g], along_z(2 + 4 * c),
        )

    def detour_on(x_first, g):
        return remote(
            detour.at[g], moved.at[g, 2] if x_first else midway.at[g, 4],
            send6.at[g], recv3.at[g, 2] if x_first else recv2.at[g, 4], along_z(2 + 4 * c),
        )

    def detour_leg(x_first, g):
        @pl.when(relay)
        def _():
            detour_out(x_first, g).wait_recv()
            detour_on(x_first, g).start()

    def copy4(g, step):
        held = lax.rem(zy - y - step + 8, 4)
        return remote(
            moved.at[g, held], landed.at[g, step],
            send4.at[g, step], recv4.at[g, step], along_y(step),
        )

    def embed(g):
        here = pl.ds(pl.multiple_of(g * chunk, chunk), chunk)
        hidden = edge_ref[here, :]
        for index in range(layers):
            hidden = layer(hidden, w_ref[index])
        first[here, :] = hidden

    def second_leg(x_first, g):
        for step in range(1, 4):
            copy1(g, step).wait_recv()
        for m in range(4):
            if far2(x_first, m) is not False:
                when(far2(x_first, m), lambda: copy2(x_first, g, m).start())
            if near2(x_first, m) is not False:

                def keep():
                    midway[g, hop2(m)] = spread[g, held2(m)]

                when(near2(x_first, m), keep)
            if m == 2 and not x_first:
                when(relay, lambda: detour_out(False, g).start())

    def third_leg(x_first, g):
        def arrive():
            for hop in range(8):
                if x_first:
                    when(True if hop % 2 else far, lambda: got2(g, hop).wait_recv())
                elif hop:
                    got2(g, hop).wait_recv()

        when(relay, arrive)
        for hop in (4, 3, 5, 2, 6, 1, 7, 0):
            if far3(x_first, hop) is not False:
                when(far3(x_first, hop), lambda: copy3(x_first, g, hop).start())
            if near3(x_first, hop) is not False:

                def keep():
                    moved[g, slot3(x_first, hop)] = midway[g, hop]

                when(near3(x_first, hop), keep)
            if hop == 4 and x_first:
                when(relay, lambda: detour_out(True, g).start())

    def fourth_leg(x_first, g):
        for slot in range(4):
            if x_first:
                when(True if slot else leaf, lambda: got3(g, slot).wait_recv())
            else:
                when(far, lambda: got3(g, slot).wait_recv())

    def sent(x_first, g):
        for m in range(4):
            when(far2(x_first, m), lambda: copy2(x_first, g, m).wait_send())
        for hop in range(8):
            if far3(x_first, hop) is not False:
                when(far3(x_first, hop), lambda: copy3(x_first, g, hop).wait_send())

        @pl.when(relay)
        def _():
            detour_out(x_first, g).wait_send()
            detour_on(x_first, g).wait_send()


    def by_kind(work, g):
        @pl.when(lax.rem(g, 2) == 0)
        def _():
            work(False, g)

        @pl.when(lax.rem(g, 2) == 1)
        def _():
            work(True, g)

    def stage(i, carry):
        @pl.when(i < CHUNKS)
        def _():
            for step in range(1, 4):
                copy1(i, step).start()
            own = pl.ds(pl.multiple_of(i * chunk + y * piece, piece), piece)
            spread[i, 0] = first[own, :]

        @pl.when(i + 1 < CHUNKS)
        def _():
            embed(i + 1)

        def run(g, leg, kinds=(False, True)):
            for x_first in kinds:

                @pl.when((g >= 0) & (g < CHUNKS) & (lax.rem(g + 2, 2) == int(x_first)))
                def _():
                    leg(x_first, g)

        run(i - LAGS[0], second_leg)
        run(i - LAGS[0] - 1, detour_leg, (False,))
        run(i - sum(LAGS[:2]), third_leg)
        run(i - sum(LAGS[:2]) - 1, detour_leg, (True,))

        @pl.when(i == 2)
        def _():
            for item in load_rest:
                item.start()
            total[...] = jnp.zeros_like(total)

        @pl.when(i == CHUNKS + 3)
        def _():
            for item in load_rest:
                item.wait()
            atoms = atom_ref[...]
            owner = jnp.zeros_like(atoms)
            for k in range(owner_ref.shape[1]):
                owner = jnp.where(atoms // SUB == k, owner_ref[:, k : k + 1], owner)
            edge = lax.broadcasted_iota(jnp.int32, atoms.shape, 1)
            place[...] = jnp.where(edge < count_ref[...], owner, -1)
            row = lax.broadcasted_iota(jnp.int32, (SUB, edges), 0)
            match[...] = jnp.where(row == atoms % SUB, 1.0, 0.0).astype(BF16)

        g = i - sum(LAGS[:3])

        @pl.when((g >= 0) & (g < CHUNKS))
        def _():
            by_kind(fourth_leg, g)
            for step in range(1, 4):
                copy4(g, step).start()
            landed[g, 0] = moved[g, lax.rem(zy - y + 4, 4)]

        @pl.when(i >= sum(LAGS))
        def _():
            g = i - sum(LAGS)
            for step in range(1, 4):
                copy4(g, step).wait_recv()
            block = landed[g].reshape(chunk, width)
            lane = lax.broadcasted_iota(jnp.int32, (1, chunk), 1)
            slot, offset = lane // piece, lane % piece
            origin = g * chunk + ((y + 4 - slot) % 4) * piece + offset

            def picked(some):
                wide = jnp.concatenate([rev_wide[some, :]] * (chunk // 128), axis=1)
                choose = jnp.where(wide == origin, 1.0, 0.0).astype(BF16)
                return total[some, :] + jnp.dot(choose, block, preferred_element_type=F32)

            def add(t, carry):
                some = pl.ds(pl.multiple_of(t * 1024, 1024), 1024)
                total[some, :] = picked(some)
                return carry

            def tell(t, carry):
                some = pl.ds(pl.multiple_of(t * 1024, 1024), 1024)
                both = first[some, :].astype(F32) + total[some, :]
                hidden = (both * HALF_ROOT).astype(BF16)
                for index in range(layers):
                    hidden = layer(hidden, w_post_ref[index])
                message[some, :] = jnp.dot(
                    hidden, w_out_ref[...], preferred_element_type=F32
                ).astype(BF16)
                return carry

            lax.fori_loop(0, rows // 1024, add, 0)

            @pl.when(g == CHUNKS - 1)
            def _():
                lax.fori_loop(0, rows // 1024, tell, 0)

        return carry

    load_head.wait()
    load_w.wait()
    load_tail.start()
    embed(0)
    load_rev.wait()

    def widen(t, carry):
        part = pl.ds(pl.multiple_of(t * 128, 128), 128)
        rev_wide[part, :] = jnp.broadcast_to(rev_ref[:, part], (128, 128)).T
        return carry

    lax.fori_loop(0, rows // 128, widen, 0)
    load_tail.wait()
    pl.semaphore_wait(barrier, jnp.where(settled, 12, 14))
    lax.fori_loop(0, CHUNKS + sum(LAGS), stage, 0)

    def owner_copy(out, into, send, recv, index, device):
        return pltpu.make_async_remote_copy(
            src_ref=out.at[index], dst_ref=into.at[index],
            send_sem=send.at[index], recv_sem=recv.at[index],
            device_id=device, device_id_type=MESH,
        )

    def pair_copy(hop):
        return owner_copy(pair_out, pair_in, pair_send, pair_recv, hop, other)

    def left_y(dy, dx):
        return owner_copy(
            left_y_out, left_y_in, left_y_send, left_y_recv, 2 * (dy - 1) + dx, along_y(dy)
        )

    def left_x():
        return owner_copy(left_x_out, left_x_in, left_x_send, left_x_recv, 0, across)

    def right_x(dy):
        return owner_copy(right_x_out, right_x_in, right_x_send, right_x_recv, dy, across)

    def right_y(dy):
        return owner_copy(right_y_out, right_y_in, right_y_send, right_y_recv, dy - 1, along_y(dy))

    def compute(hop):
        dy, dx = HOPS[hop]
        position = 4 * lax.rem(y + dy, 4) + 2 * lax.rem(xh + dx, 2)

        def chosen(at):
            return match[...] * jnp.where(place[...] == at, 1.0, 0.0).astype(BF16)

        select = jnp.concatenate([chosen(position + 1 - c), chosen(position + c)], axis=0)
        sums = jnp.dot(select, message[...], preferred_element_type=F32)
        pair_out[hop] = sums[:SUB].astype(BF16)
        pair_copy(hop).start()
        mine[hop % 2] = sums[SUB:]

    def pass_on(hop):
        dy, dx = HOPS[hop]
        pair_copy(hop).wait_recv()
        chip_sum = mine[hop % 2] + pair_in[hop].astype(F32)
        if dy:
            left_y_out[2 * (dy - 1) + dx] = chip_sum[:, :half].astype(BF16)
            left_y(dy, dx).start()
        else:
            left_keep[dx] = chip_sum[:, :half]
        if dx:
            right_x_out[dy] = chip_sum[:, half:].astype(BF16)
            right_x(dy).start()
        else:
            right_keep[dy] = chip_sum[:, half:]

    def turn_right(dy):
        right_x(dy).wait_recv()
        right_y_out[dy - 1] = (right_keep[dy] + right_x_in[dy].astype(F32)).astype(BF16)
        right_y(dy).start()

    def gathered(dx):
        value = left_keep[dx]
        for dy in (2, 1, 3):
            left_y(dy, dx).wait_recv()
            value = value + left_y_in[2 * (dy - 1) + dx].astype(F32)
        return value

    compute(0)
    for hop in range(1, 8):
        compute(hop)
        pass_on(hop - 1)
        if hop >= 6:
            turn_right(HOPS[hop - 2][0])
    left_x_out[0] = gathered(1).astype(BF16)
    left_x().start()
    pass_on(7)
    turn_right(HOPS[6][0])
    left_sum = gathered(0)
    right_x(0).wait_recv()
    right_sum = right_keep[0] + right_x_in[0].astype(F32)
    for dy in (1, 3, 2):
        right_y(dy).wait_recv()
        right_sum = right_sum + right_y_in[dy - 1].astype(F32)
    out_ref[:, half:] = right_sum.astype(BF16)
    left_x().wait_recv()
    out_ref[:, :half] = (left_sum + left_x_in[0].astype(F32)).astype(BF16)

    def settle(g, carry):
        for step in range(1, 4):
            copy1(g, step).wait_send()
            copy4(g, step).wait_send()
        by_kind(sent, g)
        return carry

    lax.fori_loop(0, CHUNKS, settle, 0)
    for hop in range(8):
        pair_copy(hop).wait_send()
    left_x().wait_send()
    for dy in range(4):
        right_x(dy).wait_send()
    for dy in (1, 2, 3):
        right_y(dy).wait_send()
        for dx in (0, 1):
            left_y(dy, dx).wait_send()


def edge_block(*operands):
    edge, w_pre, rev, w_post, w_out, atoms, count, owners = operands
    rows, width = edge.shape
    message_width = w_out.shape[1]
    piece = rows // CHUNKS // 4
    pieces = lambda n: pltpu.VMEM((CHUNKS, n, piece, width), BF16)
    grid_sems = lambda n: pltpu.SemaphoreType.DMA((CHUNKS, n))
    whole = lambda n, kind=BF16: pltpu.VMEM((n, SUB, message_width), kind)
    halves = lambda n, kind=BF16: pltpu.VMEM((n, SUB, message_width // 2), kind)
    sems = lambda n: pltpu.SemaphoreType.DMA((n,))
    return pl.pallas_call(
        edge_kernel,
        name="edge_block",
        out_shape=jax.ShapeDtypeStruct((SUB, message_width), BF16),
        in_specs=[pl.BlockSpec(memory_space=pltpu.HBM)] * len(operands),
        out_specs=pl.BlockSpec(memory_space=pltpu.VMEM),
        scratch_shapes=[
            *(pltpu.VMEM(operand.shape, operand.dtype) for operand in operands),
            sems(9),
            pltpu.VMEM((rows, width), BF16),
            pieces(4), pieces(8), pieces(4), pieces(4),
            pltpu.VMEM((CHUNKS, piece, width), BF16),
            pltpu.VMEM((rows, width), F32),
            pltpu.VMEM((rows, 128), jnp.int32),
            *(grid_sems(n) for n in (4, 4, 4, 8, 8, 4, 4, 4)),
            sems(CHUNKS), sems(CHUNKS),
            pltpu.VMEM((rows, message_width), BF16),
            pltpu.VMEM((SUB, rows), BF16),
            pltpu.VMEM(atoms.shape, jnp.int32),
            whole(8), whole(8), whole(2, F32),
            halves(6), halves(6), halves(1), halves(1), halves(2, F32),
            halves(4), halves(4), halves(3), halves(3), halves(4, F32),
            *(sems(n) for n in (8, 8, 6, 6, 1, 1, 4, 4, 3, 3)),
        ],
        compiler_params=pltpu.CompilerParams(
            collective_id=0, has_side_effects=True, vmem_limit_bytes=VMEM_BYTES
        ),
    )(*operands)


def shards(edge_feat, tile_counts, reverse_rows, incidence, owner_map, w_pre, w_post, w_out):
    return edge_block(
        edge_feat[0, 0], w_pre, reverse_rows[0], w_post, w_out,
        incidence[0], tile_counts, owner_map,
    )[None]


def solution(mesh):
    finer = Mesh(mesh.devices.reshape(4, 2, 2, 8, 2), ("y", "xh", "c", "z", "xl"))
    return jax.shard_map(
        shards,
        mesh=finer,
        in_specs=(
            P(SRC, TGT, None, None),
            P(SRC, TGT),
            P(SRC, TGT, None),
            P(SRC, TGT, None),
            P(TGT, None),
            P(),
            P(),
            P(),
        ),
        out_specs=P(TGT, SRC, None),
        check_vma=False,
    )
```

```python
import jax
import jax.numpy as jnp
from jax import lax
from jax.experimental import pallas as pl
from jax.experimental.pallas import tpu as pltpu
from jax.sharding import Mesh
from jax.sharding import PartitionSpec as P

SUB = 256
HALF_ROOT = 0.7071067811865476
MESH = pl.DeviceIdType.MESH
SRC = ("y", "xh", "c")
TGT = ("z", "xl")
CHUNKS = 8
LAGS = (2, 3, 3, 2)
VMEM_BYTES = 62 << 20
F32 = jnp.float32
BF16 = jnp.bfloat16


def layer(hidden, weight):
    half = jnp.dot(hidden, weight, preferred_element_type=F32) * 0.5
    silu = half + half * jnp.tanh(half)
    return ((hidden.astype(F32) + silu) * HALF_ROOT).astype(BF16)


def where_am_i():
    return tuple(lax.axis_index(name) for name in ("y", "xh", "c", "z", "xl"))


HOPS = ((2, 1), (1, 1), (3, 1), (0, 1), (2, 0), (1, 0), (3, 0), (0, 0))


def edge_kernel(
    edge_hbm, w_hbm, rev_hbm, w_post_hbm, w_out_hbm, atom_hbm, count_hbm, owner_hbm, out_ref,
    edge_ref, w_ref, rev_ref, w_post_ref, w_out_ref, atom_ref, count_ref, owner_ref, load, first, spread, midway, moved, landed, detour, total, rev_wide,
    send1, recv1, send2, recv2, send3, recv3, send4, recv4, recv5, send6,
    message, match, place, pair_out, pair_in, mine,
    left_y_out, left_y_in, left_x_out, left_x_in, left_keep,
    right_x_out, right_x_in, right_y_out, right_y_in, right_keep,
    pair_send, pair_recv, left_y_send, left_y_recv, left_x_send, left_x_recv,
    right_x_send, right_x_recv, right_y_send, right_y_recv,
):
    y, xh, c, z, xl = where_am_i()
    zy, z0 = z // 2, lax.rem(z, 2)
    odd = lax.rem(xh + z0, 2)
    relay = odd == 0
    settled = c == xl
    alone = relay & settled
    far = jnp.logical_not(alone)
    leaf = jnp.logical_not(relay)
    rows, width = edge_ref.shape
    layers = w_ref.shape[0]
    chunk = rows // CHUNKS
    piece = chunk // 4

    edges, message_width = message.shape
    half = message_width // 2
    other = (y, xh, 1 - c, z, xl)
    across = (y, 1 - xh, c, z, xl)

    def along_y(step):
        return (lax.rem(y + step, 4), xh, c, z, xl)

    def along_z(step):
        return (y, xh, c, lax.rem(z + step, 8), xl)

    def along_x(flip):
        return (y, lax.rem(xh + flip, 2), xl, z, c)

    def greet(device):
        pl.semaphore_signal(barrier, inc=1, device_id=device, device_id_type=MESH)

    barrier = pltpu.get_barrier_semaphore()
    for step in range(1, 4):
        greet(along_y(step))
    for step in range(1, 8):
        greet(along_z(step))
    greet(along_x(1))
    greet(other)

    @pl.when(jnp.logical_not(settled))
    def _():
        greet(along_x(0))
        greet(across)

    head, tail = pl.ds(0, chunk), pl.ds(chunk, rows - chunk)
    load_w = pltpu.make_async_copy(w_hbm, w_ref, load.at[0])
    load_head = pltpu.make_async_copy(edge_hbm.at[head], edge_ref.at[head], load.at[1])
    load_tail = pltpu.make_async_copy(edge_hbm.at[tail], edge_ref.at[tail], load.at[2])
    load_rev = pltpu.make_async_copy(rev_hbm, rev_ref, load.at[3])
    load_rest = [
        pltpu.make_async_copy(out, into, load.at[4 + index])
        for index, (out, into) in enumerate((
            (w_post_hbm, w_post_ref), (w_out_hbm, w_out_ref), (atom_hbm, atom_ref),
            (count_hbm, count_ref), (owner_hbm, owner_ref),
        ))
    ]
    for item in (load_head, load_w, load_rev):
        item.start()

    def remote(src, dst, send, recv, device):
        return pltpu.make_async_remote_copy(
            src_ref=src, dst_ref=dst, send_sem=send, recv_sem=recv,
            device_id=device, device_id_type=MESH,
        )

    def when(condition, work):
        if condition is True:
            work()
        else:
            pl.when(condition)(work)

    def copy1(g, step):
        start = pl.multiple_of(g * chunk + lax.rem(y + step, 4) * piece, piece)
        return remote(
            first.at[pl.ds(start, piece)], spread.at[g, step],
            send1.at[g, step], recv1.at[g, step], along_y(step),
        )

    def hop2(m):
        return 2 * m + odd

    def held2(m):
        return lax.rem(y + 8 - lax.rem(z + hop2(m), 8) // 2, 4)

    def copy2(x_first, g, m):
        return remote(
            spread.at[g, held2(m)], midway.at[g, hop2(m)],
            send2.at[g, m], recv2.at[g, hop2(m)],
            along_x(odd) if x_first else along_z(hop2(m)),
        )

    def far2(x_first, m):
        return far if x_first else (leaf if m in (0, 2) else True)

    def near2(x_first, m):
        return alone if x_first else (relay if m == 0 else False)

    def slot3(x_first, hop):
        turn = z0 if x_first else 1 - z0
        return lax.rem((hop + (hop % 2) * turn) // 2, 4)

    def copy3(x_first, g, hop):
        return remote(
            midway.at[g, hop], moved.at[g, slot3(x_first, hop)],
            send3.at[g, hop], recv3.at[g, slot3(x_first, hop)],
            along_z(hop) if x_first else along_x(hop % 2),
        )

    def far3(x_first, hop):
        if x_first:
            return relay if hop % 4 else False
        return relay if hop % 2 else relay & far

    def near3(x_first, hop):
        if x_first:
            return False if hop else relay
        return False if hop % 2 else alone

    def got2(g, hop):
        return remote(
            spread.at[g, 0], midway.at[g, hop], send2.at[g, 0], recv2.at[g, hop], along_y(1)
        )

    def got3(g, slot):
        return remote(
            midway.at[g, 0], moved.at[g, slot], send3.at[g, 0], recv3.at[g, slot], along_y(1)
        )

    def detour_out(x_first, g):
        return remote(
            midway.at[g, 4] if x_first else spread.at[g, held2(2)], detour.at[g],
            send3.at[g, 4] if x_first else send2.at[g, 2], recv5.at[g], along_z(2 + 4 * c),
        )

    def detour_on(x_first, g):
        return remote(
            detour.at[g], moved.at[g, 2] if x_first else midway.at[g, 4],
            send6.at[g], recv3.at[g, 2] if x_first else recv2.at[g, 4], along_z(2 + 4 * c),
        )

    def detour_leg(x_first, g):
        @pl.when(relay)
        def _():
            detour_out(x_first, g).wait_recv()
            detour_on(x_first, g).start()

    def copy4(g, step):
        held = lax.rem(zy - y - step + 8, 4)
        return remote(
            moved.at[g, held], landed.at[g, step],
            send4.at[g, step], recv4.at[g, step], along_y(step),
        )

    def embed(g):
        here = pl.ds(pl.multiple_of(g * chunk, chunk), chunk)
        hidden = edge_ref[here, :]
        for index in range(layers):
            hidden = layer(hidden, w_ref[index])
        first[here, :] = hidden

    def second_leg(x_first, g):
        for step in range(1, 4):
            copy1(g, step).wait_recv()
        for m in range(4):
            if far2(x_first, m) is not False:
                when(far2(x_first, m), lambda: copy2(x_first, g, m).start())
            if near2(x_first, m) is not False:

                def keep():
                    midway[g, hop2(m)] = spread[g, held2(m)]

                when(near2(x_first, m), keep)
            if m == 2 and not x_first:
                when(relay, lambda: detour_out(False, g).start())

    def third_leg(x_first, g):
        def arrive():
            for hop in range(8):
                if x_first:
                    when(True if hop % 2 else far, lambda: got2(g, hop).wait_recv())
                elif hop:
                    got2(g, hop).wait_recv()

        when(relay, arrive)
        for hop in (4, 3, 5, 2, 6, 1, 7, 0):
            if far3(x_first, hop) is not False:
                when(far3(x_first, hop), lambda: copy3(x_first, g, hop).start())
            if near3(x_first, hop) is not False:

                def keep():
                    moved[g, slot3(x_first, hop)] = midway[g, hop]

                when(near3(x_first, hop), keep)
            if hop == 4 and x_first:
                when(relay, lambda: detour_out(True, g).start())

    def fourth_leg(x_first, g):
        for slot in range(4):
            if x_first:
                when(True if slot else leaf, lambda: got3(g, slot).wait_recv())
            else:
                when(far, lambda: got3(g, slot).wait_recv())

    def sent(x_first, g):
        for m in range(4):
            when(far2(x_first, m), lambda: copy2(x_first, g, m).wait_send())
        for hop in range(8):
            if far3(x_first, hop) is not False:
                when(far3(x_first, hop), lambda: copy3(x_first, g, hop).wait_send())

        @pl.when(relay)
        def _():
            detour_out(x_first, g).wait_send()
            detour_on(x_first, g).wait_send()


    def by_kind(work, g):
        @pl.when(lax.rem(g, 2) == 0)
        def _():
            work(False, g)

        @pl.when(lax.rem(g, 2) == 1)
        def _():
            work(True, g)

    def stage(i, carry):
        @pl.when(i < CHUNKS)
        def _():
            for step in range(1, 4):
                copy1(i, step).start()
            own = pl.ds(pl.multiple_of(i * chunk + y * piece, piece), piece)
            spread[i, 0] = first[own, :]

        @pl.when(i + 1 < CHUNKS)
        def _():
            embed(i + 1)

        def run(g, leg, kinds=(False, True)):
            for x_first in kinds:

                @pl.when((g >= 0) & (g < CHUNKS) & (lax.rem(g + 2, 2) == int(x_first)))
                def _():
                    leg(x_first, g)

        run(i - LAGS[0], second_leg)
        run(i - LAGS[0] - 1, detour_leg, (False,))
        run(i - sum(LAGS[:2]), third_leg)
        run(i - sum(LAGS[:2]) - 1, detour_leg, (True,))

        @pl.when(i == 2)
        def _():
            for item in load_rest:
                item.start()
            total[...] = jnp.zeros_like(total)

        @pl.when(i == CHUNKS + 3)
        def _():
            for item in load_rest:
                item.wait()
            atoms = atom_ref[...]
            owner = jnp.zeros_like(atoms)
            for k in range(owner_ref.shape[1]):
                owner = jnp.where(atoms // SUB == k, owner_ref[:, k : k + 1], owner)
            edge = lax.broadcasted_iota(jnp.int32, atoms.shape, 1)
            place[...] = jnp.where(edge < count_ref[...], owner, -1)
            row = lax.broadcasted_iota(jnp.int32, (SUB, edges), 0)
            match[...] = jnp.where(row == atoms % SUB, 1.0, 0.0).astype(BF16)

        g = i - sum(LAGS[:3])

        @pl.when((g >= 0) & (g < CHUNKS))
        def _():
            by_kind(fourth_leg, g)
            for step in range(1, 4):
                copy4(g, step).start()
            landed[g, 0] = moved[g, lax.rem(zy - y + 4, 4)]

        @pl.when(i >= sum(LAGS))
        def _():
            g = i - sum(LAGS)
            for step in range(1, 4):
                copy4(g, step).wait_recv()
            block = landed[g].reshape(chunk, width)
            lane = lax.broadcasted_iota(jnp.int32, (1, chunk), 1)
            slot, offset = lane // piece, lane % piece
            origin = g * chunk + ((y + 4 - slot) % 4) * piece + offset

            def picked(some):
                wide = jnp.concatenate([rev_wide[some, :]] * (chunk // 128), axis=1)
                choose = jnp.where(wide == origin, 1.0, 0.0).astype(BF16)
                return total[some, :] + jnp.dot(choose, block, preferred_element_type=F32)

            def add(t, carry):
                some = pl.ds(pl.multiple_of(t * 2048, 2048), 2048)
                total[some, :] = picked(some)
                return carry

            def tell(t, carry):
                some = pl.ds(pl.multiple_of(t * 1024, 1024), 1024)
                both = first[some, :].astype(F32) + total[some, :]
                hidden = (both * HALF_ROOT).astype(BF16)
                for index in range(layers):
                    hidden = layer(hidden, w_post_ref[index])
                message[some, :] = jnp.dot(
                    hidden, w_out_ref[...], preferred_element_type=F32
                ).astype(BF16)
                return carry

            lax.fori_loop(0, rows // 2048, add, 0)

            @pl.when(g == CHUNKS - 1)
            def _():
                lax.fori_loop(0, rows // 1024, tell, 0)

        return carry

    load_head.wait()
    load_w.wait()
    load_tail.start()
    embed(0)
    load_rev.wait()

    def widen(t, carry):
        part = pl.ds(pl.multiple_of(t * 128, 128), 128)
        rev_wide[part, :] = jnp.broadcast_to(rev_ref[:, part], (128, 128)).T
        return carry

    lax.fori_loop(0, rows // 128, widen, 0)
    load_tail.wait()
    pl.semaphore_wait(barrier, jnp.where(settled, 12, 14))
    lax.fori_loop(0, CHUNKS + sum(LAGS), stage, 0)

    def owner_copy(out, into, send, recv, index, device):
        return pltpu.make_async_remote_copy(
            src_ref=out.at[index], dst_ref=into.at[index],
            send_sem=send.at[index], recv_sem=recv.at[index],
            device_id=device, device_id_type=MESH,
        )

    def pair_copy(hop):
        return owner_copy(pair_out, pair_in, pair_send, pair_recv, hop, other)

    def left_y(dy, dx):
        return owner_copy(
            left_y_out, left_y_in, left_y_send, left_y_recv, 2 * (dy - 1) + dx, along_y(dy)
        )

    def left_x():
        return owner_copy(left_x_out, left_x_in, left_x_send, left_x_recv, 0, across)

    def right_x(dy):
        return owner_copy(right_x_out, right_x_in, right_x_send, right_x_recv, dy, across)

    def right_y(dy):
        return owner_copy(right_y_out, right_y_in, right_y_send, right_y_recv, dy - 1, along_y(dy))

    def compute(hop):
        dy, dx = HOPS[hop]
        position = 4 * lax.rem(y + dy, 4) + 2 * lax.rem(xh + dx, 2)

        def chosen(at):
            return match[...] * jnp.where(place[...] == at, 1.0, 0.0).astype(BF16)

        select = jnp.concatenate([chosen(position + 1 - c), chosen(position + c)], axis=0)
        sums = jnp.dot(select, message[...], preferred_element_type=F32)
        pair_out[hop] = sums[:SUB].astype(BF16)
        pair_copy(hop).start()
        mine[hop % 2] = sums[SUB:]

    def pass_on(hop):
        dy, dx = HOPS[hop]
        pair_copy(hop).wait_recv()
        chip_sum = mine[hop % 2] + pair_in[hop].astype(F32)
        if dy:
            left_y_out[2 * (dy - 1) + dx] = chip_sum[:, :half].astype(BF16)
            left_y(dy, dx).start()
        else:
            left_keep[dx] = chip_sum[:, :half]
        if dx:
            right_x_out[dy] = chip_sum[:, half:].astype(BF16)
            right_x(dy).start()
        else:
            right_keep[dy] = chip_sum[:, half:]

    def turn_right(dy):
        right_x(dy).wait_recv()
        right_y_out[dy - 1] = (right_keep[dy] + right_x_in[dy].astype(F32)).astype(BF16)
        right_y(dy).start()

    def gathered(dx):
        value = left_keep[dx]
        for dy in (2, 1, 3):
            left_y(dy, dx).wait_recv()
            value = value + left_y_in[2 * (dy - 1) + dx].astype(F32)
        return value

    compute(0)
    for hop in range(1, 8):
        compute(hop)
        pass_on(hop - 1)
        if hop >= 6:
            turn_right(HOPS[hop - 2][0])
    left_x_out[0] = gathered(1).astype(BF16)
    left_x().start()
    pass_on(7)
    turn_right(HOPS[6][0])
    left_sum = gathered(0)
    right_x(0).wait_recv()
    right_sum = right_keep[0] + right_x_in[0].astype(F32)
    for dy in (1, 3, 2):
        right_y(dy).wait_recv()
        right_sum = right_sum + right_y_in[dy - 1].astype(F32)
    out_ref[:, half:] = right_sum.astype(BF16)
    left_x().wait_recv()
    out_ref[:, :half] = (left_sum + left_x_in[0].astype(F32)).astype(BF16)

    def settle(g, carry):
        for step in range(1, 4):
            copy1(g, step).wait_send()
            copy4(g, step).wait_send()
        by_kind(sent, g)
        return carry

    lax.fori_loop(0, CHUNKS, settle, 0)
    for hop in range(8):
        pair_copy(hop).wait_send()
    left_x().wait_send()
    for dy in range(4):
        right_x(dy).wait_send()
    for dy in (1, 2, 3):
        right_y(dy).wait_send()
        for dx in (0, 1):
            left_y(dy, dx).wait_send()


def edge_block(*operands):
    edge, w_pre, rev, w_post, w_out, atoms, count, owners = operands
    rows, width = edge.shape
    message_width = w_out.shape[1]
    piece = rows // CHUNKS // 4
    pieces = lambda n: pltpu.VMEM((CHUNKS, n, piece, width), BF16)
    grid_sems = lambda n: pltpu.SemaphoreType.DMA((CHUNKS, n))
    whole = lambda n, kind=BF16: pltpu.VMEM((n, SUB, message_width), kind)
    halves = lambda n, kind=BF16: pltpu.VMEM((n, SUB, message_width // 2), kind)
    sems = lambda n: pltpu.SemaphoreType.DMA((n,))
    return pl.pallas_call(
        edge_kernel,
        name="edge_block",
        out_shape=jax.ShapeDtypeStruct((SUB, message_width), BF16),
        in_specs=[pl.BlockSpec(memory_space=pltpu.HBM)] * len(operands),
        out_specs=pl.BlockSpec(memory_space=pltpu.VMEM),
        scratch_shapes=[
            *(pltpu.VMEM(operand.shape, operand.dtype) for operand in operands),
            sems(9),
            pltpu.VMEM((rows, width), BF16),
            pieces(4), pieces(8), pieces(4), pieces(4),
            pltpu.VMEM((CHUNKS, piece, width), BF16),
            pltpu.VMEM((rows, width), F32),
            pltpu.VMEM((rows, 128), jnp.int32),
            *(grid_sems(n) for n in (4, 4, 4, 8, 8, 4, 4, 4)),
            sems(CHUNKS), sems(CHUNKS),
            pltpu.VMEM((rows, message_width), BF16),
            pltpu.VMEM((SUB, rows), BF16),
            pltpu.VMEM(atoms.shape, jnp.int32),
            whole(8), whole(8), whole(2, F32),
            halves(6), halves(6), halves(1), halves(1), halves(2, F32),
            halves(4), halves(4), halves(3), halves(3), halves(4, F32),
            *(sems(n) for n in (8, 8, 6, 6, 1, 1, 4, 4, 3, 3)),
        ],
        compiler_params=pltpu.CompilerParams(
            collective_id=0, has_side_effects=True, vmem_limit_bytes=VMEM_BYTES
        ),
    )(*operands)


def shards(edge_feat, tile_counts, reverse_rows, incidence, owner_map, w_pre, w_post, w_out):
    return edge_block(
        edge_feat[0, 0], w_pre, reverse_rows[0], w_post, w_out,
        incidence[0], tile_counts, owner_map,
    )[None]


def solution(mesh):
    finer = Mesh(mesh.devices.reshape(4, 2, 2, 8, 2), ("y", "xh", "c", "z", "xl"))
    return jax.shard_map(
        shards,
        mesh=finer,
        in_specs=(
            P(SRC, TGT, None, None),
            P(SRC, TGT),
            P(SRC, TGT, None),
            P(SRC, TGT, None),
            P(TGT, None),
            P(),
            P(),
            P(),
        ),
        out_specs=P(TGT, SRC, None),
        check_vma=False,
    )
```
